32 devices in a mesh: groups: 2 (over y), prefix: 4 (over z), heads: 2 (over x), sub: 2 (over core).
Axes of the slice: x: 2, y: 2, z: 4, core: 2. Of those that a mesh axis runs over, the one named last changes fastest.
Arguments:
- queries: bfloat16 [256, 8, 16, 128], P(('groups', 'prefix'), 'heads', 'sub'), parts along dimension 0, may hold values from -150 to 150
- prefix_keys: bfloat16 [16384, 8, 128], P(('groups', 'prefix'), 'heads'), parts along dimension 0, may hold values from -8 to 8
- prefix_values: bfloat16 [16384, 8, 128], P(('groups', 'prefix'), 'heads'), parts along dimension 0, may hold values from -9 to 9
- suffix_keys: bfloat16 [64, 1024, 8, 128], P(('groups', 'prefix'), None, 'heads'), parts along dimension 0, may hold values from -12 to 12
- suffix_values: bfloat16 [64, 1024, 8, 128], P(('groups', 'prefix'), None, 'heads'), parts along dimension 0, may hold values from -2 to 1
- accepted: int32 [64], P('groups'), parts along dimension 0, may hold values from 1 to 8, 128 in all
- cache_slot: int32 [64], P('groups'), parts along dimension 0, may hold values from 0 to 31, each once
- history: int32 [64], P('groups'), parts along dimension 0, may hold values from 128 to 1016
Outputs:
- attended: bfloat16 [256, 8, 16, 128], P(('groups', 'prefix'), 'heads', 'sub'), parts along dimension 0
The draws below stay inside these ranges and needn't reach their ends.
There are 2 independent parts, one for each index of `groups`. The reference program is written for one: setup_inputs(seed, part) draws one part's arguments, and reference() takes and returns one part's arrays. A program takes and returns all parts, laid end to end along the dimension named above; each array names one. Nothing has to cross between parts.
Inputs may be any that keep to these rules, and one draw needn't show every extreme that they name: `accepted`: the counts sum to 128, and the largest count is 8. `cache_slot`: each slot is named by exactly one request; slot s lies on index s // 8 of prefix, at place s % 8.
All inputs are finite; a program needn't handle non-finite values.
Results may differ from the reference program's by a relative error of at most 0.005.
Values may be sent and summed in bfloat16 or wider, within the bound.
A program may use at most 128 MiB of HBM per device.

```python
import math
import jax
import jax.numpy as jnp
import numpy as np
from jax import lax

KVH = 8
HD = 128
GROUP = 16
MOST = 8
SLEN = 1024
PLEN = 8192
REQUESTS = 32
TOKENS = 128


def shared_keys(key):
    keys_drawn = jax.random.normal(jax.random.fold_in(key, 7), (PLEN, KVH, HD), jnp.float32)
    return keys_drawn


def draw_prefix_keys(key, part):
    return shared_keys(key).astype(jnp.bfloat16)


def draw_queries(key, part):
    fresh = jax.random.normal(jax.random.fold_in(key, 9), (TOKENS, KVH, GROUP, HD), jnp.float32)
    return fresh.astype(jnp.bfloat16)


def draw_prefix_values(key, part):
    noise = jax.random.normal(jax.random.fold_in(key, 21), (PLEN, KVH, HD), jnp.float32)
    shifts = jax.random.uniform(jax.random.fold_in(key, 22), (PLEN // 32, KVH, HD), jnp.float32, -1.5, 1.5)
    shifts = jnp.repeat(shifts, 32, axis=0)
    return jnp.clip(noise + shifts, -9.0, 9.0).astype(jnp.bfloat16)


def set_ends(array, stream_key, low, high):
    longest = array.shape.index(max(array.shape))
    spots = []
    for shift in (0, 1):
        where = [jax.random.randint(jax.random.fold_in(stream_key, axis), (), 0, length) for axis, length in enumerate(array.shape)]
        where[longest] = (where[longest] + shift) % array.shape[longest]
        spots.append(tuple(where))
    return array.at[spots[0]].set(low).at[spots[1]].set(high)


def levels(stream_key, extent, split, low, high):
    def one(position, parts):
        steps = jax.random.uniform(jax.random.fold_in(jax.random.fold_in(stream_key, 6), position), (parts,), jnp.float32, low / len(split), high / len(split))
        return jnp.repeat(jnp.exp(steps), extent[position] // parts).reshape((-1,) + (1,) * (len(extent) - position - 1))

    loudness = one(*split[0])
    for cut in split[1:]:
        loudness = loudness * one(*cut)
    return loudness


def length_profile(amount, total, most, skew):
    loads = [(1 << 20) // math.isqrt(grade ** skew) + 1 for grade in range(2, amount + 1)]
    spare, counts = total - most - (amount - 1), [1] * (amount - 1)
    while spare > 0:
        candidates = [i for i in range(amount - 1) if counts[i] < most]
        whole, remaining = sum([loads[i] for i in candidates]), spare
        for i in candidates:
            extra = min(most - counts[i], max(1, remaining * loads[i] // whole), spare)
            counts[i] = counts[i] + extra
            spare = spare - extra
    return np.array([most] + counts)


def uneven(stream_key, amount, total, most, slope):
    if amount == 2:
        one = jax.random.randint(stream_key, (), max(1, total - most), min(most, total - 1) + 1)
        return jnp.stack([one, total - one])
    sizes = jnp.asarray(length_profile(amount, total, most, slope), jnp.int32)
    couples = (amount - 1) // 2
    source_of, taker = sizes[1:1 + 2 * couples:2], sizes[2:2 + 2 * couples:2]
    slack = jnp.minimum(source_of - 1, most - taker)
    passed = jax.random.randint(jax.random.fold_in(stream_key, 1), (couples,), 0, 1 << 20) % (slack + 1)
    sizes = sizes.at[1:1 + 2 * couples:2].set(source_of - passed).at[2:2 + 2 * couples:2].set(taker + passed)
    return sizes[jax.random.permutation(jax.random.fold_in(stream_key, 2), amount)]


def centred(key, extent, scale, bound, shards=(), kind=jnp.bfloat16):
    loudness = levels(key, extent, shards, -0.22, 0.18) if shards else 1.0
    array = jax.random.normal(key, extent, jnp.float32) * scale * loudness
    return jnp.minimum(jnp.maximum(array, -bound), bound).astype(kind)


def setup_inputs(seed: int = 0, part: int = 0) -> dict:
    key_list = jax.random.split(jax.random.key(seed), 9)
    part_keys = jax.random.split(jax.random.fold_in(key_list[8], part), 9)
    queries = draw_queries(jax.random.fold_in(jax.random.fold_in(key_list[8], part), 71), part)
    prefix_keys = draw_prefix_keys(jax.random.fold_in(jax.random.fold_in(key_list[8], part), 71), part)
    prefix_values = draw_prefix_values(jax.random.fold_in(jax.random.fold_in(key_list[8], part), 71), part)
    suffix_keys = centred(part_keys[3], (REQUESTS, SLEN, KVH, HD), 2.0, 12.0, ((0, 4), (2, 2)))
    suffix_values = jnp.clip(-2.0 + 3.0 * jax.random.uniform(part_keys[4], (REQUESTS, SLEN, KVH, HD), jnp.float32) ** levels(part_keys[4], (REQUESTS, SLEN, KVH, HD), ((0, 4), (2, 2)), -0.2, 0.2), -2.0, 1.0).astype(jnp.bfloat16)
    accepted = uneven(part_keys[5], REQUESTS, TOKENS, MOST, 2).astype(jnp.int32)
    cache_slot = jax.random.permutation(part_keys[6], REQUESTS).astype(jnp.int32)
    history = set_ends(jax.random.randint(part_keys[7], (REQUESTS,), SLEN // 8, SLEN - MOST + 1), jax.random.fold_in(part_keys[7], 1), SLEN // 8, SLEN - MOST).astype(jnp.int32)
    return dict(queries=queries, prefix_keys=prefix_keys, prefix_values=prefix_values, suffix_keys=suffix_keys, suffix_values=suffix_values, accepted=accepted, cache_slot=cache_slot, history=history)


negative = -1e+30

def reference(queries, prefix_keys, prefix_values, suffix_keys, suffix_values, accepted, cache_slot, history):
    scaling = 1.0 / math.sqrt(HD)
    request_ends = jnp.cumsum(accepted).astype(jnp.int32)
    starts = (request_ends - accepted).astype(jnp.int32)
    row_ids = jnp.arange(TOKENS, dtype=jnp.int32)
    request_of_row = lax.optimization_barrier(jnp.sum((row_ids[:, None] >= request_ends[None, :]).astype(jnp.int32), axis=1)).astype(jnp.int32)
    place_in = row_ids - starts[request_of_row]
    key_limit = (history[request_of_row] + place_in + 1).astype(jnp.int32)
    slot_of_row = cache_slot[request_of_row].astype(jnp.int32)
    key_span = jnp.arange(SLEN, dtype=jnp.int32)
    keys_wide = prefix_keys.astype(jnp.float32)
    values_wide = prefix_values.astype(jnp.float32)

    def one_block(inputs):
        query_block, slot_block, limit_block = inputs
        query_wide = query_block.astype(jnp.float32)
        own_keys = suffix_keys[slot_block].astype(jnp.float32)
        own_values = suffix_values[slot_block].astype(jnp.float32)
        prefix_score = jnp.einsum('rkgd,skd->rkgs', query_wide, keys_wide) * scaling
        suffix_score = jnp.einsum('rkgd,rskd->rkgs', query_wide, own_keys) * scaling
        allowed = (key_span[None, :] < limit_block[:, None])[:, None, None, :]
        top = jnp.maximum(lax.optimization_barrier(jnp.max(prefix_score, axis=-1)), lax.optimization_barrier(jnp.max(jnp.where(allowed, suffix_score, negative), axis=-1)))
        prefix_weight = jnp.exp(prefix_score - top[..., None])
        suffix_weight = jnp.where(allowed, jnp.exp(suffix_score - top[..., None]), 0.0)
        denominator = lax.optimization_barrier(jnp.sum(prefix_weight, axis=-1)) + lax.optimization_barrier(jnp.sum(suffix_weight, axis=-1))
        prefix_round = lax.optimization_barrier(prefix_weight.astype(jnp.bfloat16)).astype(jnp.float32)
        suffix_round = lax.optimization_barrier(suffix_weight.astype(jnp.bfloat16)).astype(jnp.float32)
        numerator = jnp.einsum('rkgs,skd->rkgd', prefix_round, values_wide)
        numerator = numerator + jnp.einsum('rkgs,rskd->rkgd', suffix_round, own_values)
        return (numerator / denominator[..., None]).astype(jnp.bfloat16)
    block_rows = 32
    blocked = queries.reshape(TOKENS // block_rows, block_rows, KVH, GROUP, HD)
    result = lax.map(one_block, (blocked, slot_of_row.reshape(-1, block_rows), key_limit.reshape(-1, block_rows)))
    return result.reshape(TOKENS, KVH, GROUP, HD)
```

```python
import functools
import math

import jax
import jax.numpy as jnp
from jax import lax
from jax.experimental import pallas as pl
from jax.experimental.pallas import tpu as pltpu
from jax.sharding import PartitionSpec as P

MOST = 8
NEG = -1e30
LOG2E = 1.4426950408889634
VMEM = 67043328
SPARE = 12 * 1024 * 1024
MESH = pl.DeviceIdType.MESH


def nt_dot(a, b):
    return lax.dot_general(a, b, (((1,), (1,)), ((), ())), preferred_element_type=jnp.float32)


def greet(p, n):
    barrier = pltpu.get_barrier_semaphore()
    for step, there in ((-1, p > 0), (1, p < n - 1)):

        @pl.when(there)
        def _(step=step):
            pl.semaphore_signal(
                barrier, inc=1, device_id={"prefix": p + step}, device_id_type=MESH
            )

    pl.semaphore_wait(barrier, jnp.minimum(p, 1) + jnp.minimum(n - 1 - p, 1))


def grant(*held):
    kept = sum(math.prod(x.shape) * jnp.dtype(x.dtype).itemsize for x in held)
    return VMEM - kept - SPARE


def widen(raw, wide):
    wide[...] = raw.astype(jnp.float32)


def narrow(wide, h, heads):
    return wide[pl.ds(h, wide.shape[0] // heads, stride=heads), :].astype(jnp.bfloat16)


def prefix_pass(load_q, kd, vd, acc, den, top, at, scale, arrive):
    heads, plen, hd = kd.shape
    part = min(plen, 1024)
    pieces = plen // part
    stages = [(h, c) for h in range(heads) for c in range(pieces)]

    def score(stage):
        h, c = stage
        if c == 0:
            arrive(h)
        return nt_dot(load_q(h), kd[h, pl.ds(c * part, part), :])

    ready = score(stages[0])
    held = []
    for index, (h, c) in enumerate(stages):
        s = ready
        if index + 1 < len(stages):
            ready = score(stages[index + 1])
        m = jnp.max(s, axis=1, keepdims=True) * scale
        p = jnp.exp2(s * scale - m).astype(jnp.bfloat16)
        v = vd[h, pl.ds(c * part, part), :]
        pv = jnp.dot(
            p, jnp.concatenate([v, jnp.ones_like(v)], axis=1),
            preferred_element_type=jnp.float32,
        )
        held.append((m, pv))
        if c == pieces - 1:
            m, pv = held[0]
            for m_more, pv_more in held[1:]:
                joined = jnp.maximum(m, m_more)
                pv = pv * jnp.exp2(m - joined) + pv_more * jnp.exp2(m_more - joined)
                m = joined
            held = []
            _, count, gs, _ = acc.shape
            shape = (pv.shape[0] // gs, gs, hd)
            acc[h, at] = pv[:, :hd].reshape(shape)
            den[h, at] = pv[:, hd:].reshape(shape)
            top[h, at] = jnp.broadcast_to(m, (pv.shape[0], hd)).reshape(shape)


def gather_kernel(
    q_hbm, k_hbm, v_hbm, qall, acc, den, top,
    kraw, vraw, kwide, vwide, kd, vd, own_sem, raw_sem, send_sem, recv_sem, *, n, scale, pieces
):
    p = lax.axis_index("prefix")
    rows, heads, gs, hd = q_hbm.shape
    flat = k_hbm.shape[0]
    piece = flat // pieces
    unit = kwide.shape[0]

    def raw_copies(i):
        at = pl.ds(i * piece, piece)
        return (
            pltpu.make_async_copy(k_hbm.at[at], kraw.at[at], raw_sem.at[0, i]),
            pltpu.make_async_copy(v_hbm.at[at], vraw.at[at], raw_sem.at[1, i]),
        )

    def block_at(b):
        return pl.ds(b * rows, rows)

    def own_copy(h):
        return pltpu.make_async_copy(q_hbm.at[:, h], qall.at[h, block_at(p)], own_sem.at[h])

    def send(src, side, b, h):
        return pltpu.make_async_remote_copy(
            src_ref=src,
            dst_ref=qall.at[h, block_at(b)],
            send_sem=send_sem.at[side, b, h],
            recv_sem=recv_sem.at[b, h],
            device_id={"prefix": p + 1 if side == 0 else p - 1},
            device_id_type=MESH,
        )

    for i in range(pieces):
        for copy in raw_copies(i):
            copy.start()
    for h in range(heads):
        own_copy(h).start()
    greet(p, n)
    outward = ((0, p < n - 1), (1, p > 0))
    for h in range(heads):
        for side, there in outward:

            @pl.when(there)
            def _(side=side, h=h):
                send(q_hbm.at[:, h], side, p, h).start()

    for i in range(pieces):
        for copy in raw_copies(i):
            copy.wait()

        def split(u, carry, i=i):
            at = pl.ds(pl.multiple_of(i * piece + u * unit, unit), unit)
            per = unit // heads
            to = pl.ds(pl.multiple_of(i * (piece // heads) + u * per, per), per)
            widen(kraw[at], kwide)
            widen(vraw[at], vwide)
            for h in range(heads):
                kd[h, to] = narrow(kwide, h, heads)
                vd[h, to] = narrow(vwide, h, heads)
            return carry

        lax.fori_loop(0, piece // unit, split, 0)

    near = jnp.minimum(p, n - 1 - p)
    longer = jnp.where(p > n - 1 - p, -1, 1)

    def body(k, carry):
        paired = p + jnp.where(k % 2 == 1, -1, 1) * ((k + 1) // 2)
        single = p + longer * (k - near)
        b = jnp.where(k <= 2 * near, paired, single)

        def arrive(h):
            @pl.when(k == 0)
            def _():
                own_copy(h).wait()

            for side, there in outward:
                source = p - k if side == 0 else p + k
                landed = qall.at[h, block_at(source)]

                @pl.when((k > 0) & (source >= 0) & (source < n))
                def _(side=side, source=source, landed=landed, there=there):
                    send(landed, side, source, h).wait_recv()

                    @pl.when(there)
                    def _():
                        send(landed, side, source, h).start()

        def load_q(h):
            return qall[h, block_at(b)].reshape(rows * gs, hd)

        prefix_pass(load_q, kd, vd, acc, den, top, block_at(b), scale, arrive)
        return carry

    lax.fori_loop(0, n, body, 0)

    def drain(k, carry):
        for h in range(heads):
            for side, there in outward:
                source = p - k if side == 0 else p + k

                @pl.when(there & (source >= 0) & (source < n))
                def _(side=side, source=source, h=h):
                    send(qall.at[h, block_at(source)], side, source, h).wait_send()

        return carry

    lax.fori_loop(0, n, drain, 0)


def gathered(q, kf, vf, n):
    rows, heads, gs, hd = q.shape
    flat = kf.shape[0]
    plen = flat // heads
    pieces = 4
    unit = min(1024, flat // pieces)
    everything = (heads, n * rows, gs, hd)
    state = jax.ShapeDtypeStruct(everything, jnp.float32)
    vmem = pl.BlockSpec(memory_space=pltpu.VMEM)
    hbm = pl.BlockSpec(memory_space=pltpu.HBM)
    dma = pltpu.SemaphoreType.DMA
    shapes = [jax.ShapeDtypeStruct(everything, jnp.bfloat16), state, state, state]
    return pl.pallas_call(
        functools.partial(gather_kernel, n=n, scale=LOG2E / math.sqrt(hd), pieces=pieces),
        in_specs=[hbm, hbm, hbm],
        out_specs=[vmem] * 4,
        out_shape=shapes,
        scratch_shapes=[
            pltpu.VMEM((flat, hd), jnp.bfloat16),
            pltpu.VMEM((flat, hd), jnp.bfloat16),
            pltpu.VMEM((unit, hd), jnp.float32),
            pltpu.VMEM((unit, hd), jnp.float32),
            pltpu.VMEM((heads, plen, hd), jnp.bfloat16),
            pltpu.VMEM((heads, plen, hd), jnp.bfloat16),
            dma((heads,)),
            dma((2, pieces)),
            dma((2, n, heads)),
            dma((n, heads)),
        ],
        compiler_params=pltpu.CompilerParams(
            collective_id=0, has_side_effects=True, vmem_limit_bytes=grant(*shapes)
        ),
    )(q, kf, vf)


def suffix_kernel(
    accepted, cache_slot, history, qall, acc_in, den_in, top_in, sk_hbm, sv_hbm,
    acc, den, top, kbuf, vbuf, kwide, vwide, kd, vd, meta, tasks, sems, *, scale
):
    owner = lax.axis_index("prefix")
    heads, count, gs, hd = qall.shape
    slots, flat, _ = sk_hbm.shape
    depth, wide, _ = kbuf.shape
    chunk = wide // heads
    window = MOST * gs

    def find(r, start):
        amount = accepted[r]
        slot = cache_slot[r] - owner * slots

        @pl.when((slot >= 0) & (slot < slots))
        def _():
            meta[slot, 0] = start
            meta[slot, 1] = amount
            meta[slot, 2] = history[r]

        return start + amount

    lax.fori_loop(0, accepted.shape[0], find, jnp.int32(0))

    def copies(task, buf):
        slot = tasks[task, 0]
        src = pl.ds(pl.multiple_of(tasks[task, 1] * wide, wide), wide)
        return (
            pltpu.make_async_copy(sk_hbm.at[slot, src], kbuf.at[buf], sems.at[0, buf]),
            pltpu.make_async_copy(sv_hbm.at[slot, src], vbuf.at[buf], sems.at[1, buf]),
        )

    total = jnp.int32(0)
    for slot in range(slots):
        blocks = (meta[slot, 1] + meta[slot, 2] + chunk - 1) // chunk

        def put(i, at, slot=slot):
            tasks[at, 0] = slot
            tasks[at, 1] = i
            return at + 1

        total = lax.fori_loop(0, blocks, put, total)

    for ahead in range(depth - 1):

        @pl.when(ahead < total)
        def _(ahead=ahead):
            for copy in copies(ahead, ahead):
                copy.start()

    i_row = lax.broadcasted_iota(jnp.int32, (window, 1), 0) // gs
    pos = lax.broadcasted_iota(jnp.int32, (1, chunk), 1)

    def spread():
        for h in range(heads):
            kd[h] = narrow(kwide, h, heads)
            vd[h] = narrow(vwide, h, heads)

    @pl.when(total > 0)
    def _():
        for copy in copies(0, 0):
            copy.wait()
        widen(kbuf[0], kwide)
        widen(vbuf[0], vwide)
        spread()

    def body(t, carry):
        @pl.when(t + depth - 1 < total)
        def _():
            for copy in copies(t + depth - 1, lax.rem(t + depth - 1, depth)):
                copy.start()

        @pl.when(t + 1 < total)
        def _():
            for copy in copies(t + 1, lax.rem(t + 1, depth)):
                copy.wait()

        follow = lax.rem(t + 1, depth)
        widen(kbuf[follow], kwide)
        widen(vbuf[follow], vwide)

        slot = tasks[t, 0]
        base = tasks[t, 1] * chunk
        begin = meta[slot, 0]
        amount = meta[slot, 1]
        past = meta[slot, 2]
        start = jnp.minimum(begin, count - MOST)
        place = i_row + (start - begin)
        limit = jnp.where((place >= 0) & (place < amount), past + place + 1, 0) - base
        allowed = pos < limit
        rows_at = pl.ds(start, MOST)
        shape = (MOST, gs, hd)
        scores = [nt_dot(qall[h, rows_at].reshape(window, hd), kd[h]) for h in range(heads)]
        for h in range(heads):
            s = jnp.where(allowed, scores[h], NEG)
            old_top = top[h, rows_at].reshape(window, hd)
            m = jnp.maximum(old_top, jnp.max(s, axis=1, keepdims=True) * scale)
            p = jnp.exp2(s * scale - m[:, :1]).astype(jnp.bfloat16)
            v = vd[h]
            pv = jnp.dot(
                p, jnp.concatenate([v, jnp.ones_like(v)], axis=1),
                preferred_element_type=jnp.float32,
            )
            factor = jnp.exp2(old_top - m)
            top[h, rows_at] = m.reshape(shape)
            den[h, rows_at] = (
                den[h, rows_at].reshape(window, hd) * factor + pv[:, hd:]
            ).reshape(shape)
            acc[h, rows_at] = (
                acc[h, rows_at].reshape(window, hd) * factor + pv[:, :hd]
            ).reshape(shape)
        spread()
        return carry

    lax.fori_loop(0, total, body, 0)


def with_suffix(accepted, cache_slot, history, qall, acc, den, top, sk, sv):
    heads, count, gs, hd = qall.shape
    slots, flat, _ = sk.shape
    slen = flat // heads
    chunk = min(slen, 256)
    wide = chunk * heads
    depth = 4
    vmem = pl.BlockSpec(memory_space=pltpu.VMEM)
    hbm = pl.BlockSpec(memory_space=pltpu.HBM)
    smem = pl.BlockSpec(memory_space=pltpu.SMEM)
    return pl.pallas_call(
        functools.partial(suffix_kernel, scale=LOG2E / math.sqrt(hd)),
        in_specs=[smem] * 3 + [vmem] * 4 + [hbm] * 2,
        out_specs=[vmem] * 3,
        out_shape=[jax.ShapeDtypeStruct(acc.shape, jnp.float32)] * 3,
        input_output_aliases={4: 0, 5: 1, 6: 2},
        scratch_shapes=[
            pltpu.VMEM((depth, wide, hd), jnp.bfloat16),
            pltpu.VMEM((depth, wide, hd), jnp.bfloat16),
            pltpu.VMEM((wide, hd), jnp.float32),
            pltpu.VMEM((wide, hd), jnp.float32),
            pltpu.VMEM((heads, chunk, hd), jnp.bfloat16),
            pltpu.VMEM((heads, chunk, hd), jnp.bfloat16),
            pltpu.SMEM((slots, 3), jnp.int32),
            pltpu.SMEM((slots * (slen // chunk), 2), jnp.int32),
            pltpu.SemaphoreType.DMA((2, depth)),
        ],
        compiler_params=pltpu.CompilerParams(vmem_limit_bytes=grant(qall, acc, den, top)),
    )(accepted, cache_slot, history, qall, acc, den, top, sk, sv)


def reduce_kernel(
    acc, den, top, result, out_o, out_l, in_o, in_l, send_sem, recv_sem, *, n
):
    p = lax.axis_index("prefix")
    heads, count, gs, hd = acc.shape
    rows = count // n
    size = rows * gs
    groups = size // hd
    eye = lax.broadcasted_iota(jnp.int32, (1, hd, hd), 1) == lax.broadcasted_iota(
        jnp.int32, (1, hd, hd), 2
    )

    def sends(side, b, h):
        target = {"prefix": p + 1 if side == 0 else p - 1}
        return [
            pltpu.make_async_remote_copy(
                src_ref=out.at[b, h],
                dst_ref=into.at[side, b, h],
                send_sem=send_sem.at[kind, b, h],
                recv_sem=recv_sem.at[kind, side, b, h],
                device_id=target,
                device_id_type=MESH,
            )
            for kind, (out, into) in enumerate(((out_o, in_o), (out_l, in_l)))
        ]

    def own(b, h):
        at = pl.ds(b * rows, rows)
        return [ref[h, at].reshape(size, hd) for ref in (acc, den, top)]

    def joined(state, side, b, h):
        a, d, t = state
        o = in_o[side, b, h].astype(jnp.float32)
        lanes = jnp.broadcast_to(in_l[side, b, h][:, None, :], (groups, hd, hd))
        lse = jnp.sum(jnp.where(eye, lanes, 0.0), axis=2, keepdims=True).reshape(size, 1)
        m = jnp.maximum(t, lse)
        mine = jnp.exp2(t - m)
        theirs = jnp.exp2(lse - m)
        return a * mine + o * theirs, d * mine + theirs, m

    def pass_on(side, b, h, more):
        def emit(state):
            a, d, t = state
            out_o[b, h] = (a / d).astype(jnp.bfloat16)
            lse = (t + jnp.log2(d)).reshape(groups, hd, hd)
            out_l[b, h] = jnp.sum(jnp.where(eye, lse, 0.0), axis=1)

        @pl.when(more)
        def _():
            for copy in sends(side, b, h):
                copy.wait_recv()
            emit(joined(own(b, h), side, b, h))

        @pl.when(jnp.logical_not(more))
        def _():
            emit(own(b, h))

        for copy in sends(side, b, h):
            copy.start()

    greet(p, n)

    def step(j, carry):
        for h in range(heads):

            @pl.when(n - 1 - j > p)
            def _(h=h):
                pass_on(0, n - 1 - j, h, p > 0)

            @pl.when(j < p)
            def _(h=h):
                pass_on(1, j, h, p < n - 1)

        return carry

    lax.fori_loop(0, n - 1, step, 0)

    def finish(state, h):
        a, d, _ = state
        result[:, h] = (a / d).astype(result.dtype).reshape(rows, gs, hd)

    for h in range(heads):
        for side, there in ((0, p > 0), (1, p < n - 1)):

            @pl.when(there)
            def _(side=side, h=h):
                for copy in sends(side, p, h):
                    copy.wait_recv()

        @pl.when((p > 0) & (p < n - 1))
        def _(h=h):
            finish(joined(joined(own(p, h), 0, p, h), 1, p, h), h)

        @pl.when((p > 0) & (p == n - 1))
        def _(h=h):
            finish(joined(own(p, h), 0, p, h), h)

        @pl.when((p == 0) & (p < n - 1))
        def _(h=h):
            finish(joined(own(p, h), 1, p, h), h)

    def drain(j, carry):
        for h in range(heads):

            @pl.when(n - 1 - j > p)
            def _(h=h):
                for copy in sends(0, n - 1 - j, h):
                    copy.wait_send()

            @pl.when(j < p)
            def _(h=h):
                for copy in sends(1, j, h):
                    copy.wait_send()

        return carry

    lax.fori_loop(0, n - 1, drain, 0)


def reduced(acc, den, top, n):
    heads, count, gs, hd = acc.shape
    rows = count // n
    size = rows * gs
    dma = pltpu.SemaphoreType.DMA
    return pl.pallas_call(
        functools.partial(reduce_kernel, n=n),
        out_shape=jax.ShapeDtypeStruct((rows, heads, gs, hd), jnp.bfloat16),
        scratch_shapes=[
            pltpu.VMEM((n, heads, size, hd), jnp.bfloat16),
            pltpu.VMEM((n, heads, size // hd, hd), jnp.float32),
            pltpu.VMEM((2, n, heads, size, hd), jnp.bfloat16),
            pltpu.VMEM((2, n, heads, size // hd, hd), jnp.float32),
            dma((2, n, heads)),
            dma((2, 2, n, heads)),
        ],
        compiler_params=pltpu.CompilerParams(
            collective_id=1, has_side_effects=True, vmem_limit_bytes=32 * 1024 * 1024
        ),
    )(acc, den, top)


def local(
    queries, prefix_keys, prefix_values, suffix_keys, suffix_values, accepted, cache_slot, history
):
    n = lax.axis_size("prefix")
    plen, heads, hd = prefix_keys.shape
    slots, slen, _, _ = suffix_keys.shape
    kf = prefix_keys.reshape(plen * heads, hd)
    vf = prefix_values.reshape(plen * heads, hd)
    sk = suffix_keys.reshape(slots, slen * heads, hd)
    sv = suffix_values.reshape(slots, slen * heads, hd)
    qall, acc, den, top = gathered(queries, kf, vf, n)
    acc, den, top = with_suffix(accepted, cache_slot, history, qall, acc, den, top, sk, sv)
    return reduced(acc, den, top, n)


def solution(mesh):
    in_specs = (
        P(("groups", "prefix"), "heads", "sub", None),
        P(("groups", "prefix"), "heads", None),
        P(("groups", "prefix"), "heads", None),
        P(("groups", "prefix"), None, "heads", None),
        P(("groups", "prefix"), None, "heads", None),
        P("groups"),
        P("groups"),
        P("groups"),
    )
    out_specs = P(("groups", "prefix"), "heads", "sub", None)
    return jax.shard_map(local, mesh=mesh, in_specs=in_specs, out_specs=out_specs, check_vma=False)
```

```python
import functools
import math

import jax
import jax.numpy as jnp
from jax import lax
from jax.experimental import pallas as pl
from jax.experimental.pallas import tpu as pltpu
from jax.sharding import PartitionSpec as P

MOST = 8
NEG = -1e30
FLOOR = -1e29
LOG2E = 1.4426950408889634
VMEM = 67043328
STAGGER = 2
SPARE = 12 * 1024 * 1024
MESH = pl.DeviceIdType.MESH


def nt_dot(a, b):
    return lax.dot_general(a, b, (((1,), (1,)), ((), ())), preferred_element_type=jnp.float32)


def greet(p, n):
    barrier = pltpu.get_barrier_semaphore()
    for step, there in ((-1, p > 0), (1, p < n - 1)):

        @pl.when(there)
        def _(step=step):
            pl.semaphore_signal(
                barrier, inc=1, device_id={"prefix": p + step}, device_id_type=MESH
            )

    pl.semaphore_wait(barrier, jnp.minimum(p, 1) + jnp.minimum(n - 1 - p, 1))


def grant(*held):
    kept = sum(math.prod(x.shape) * jnp.dtype(x.dtype).itemsize for x in held)
    return VMEM - kept - SPARE


def widen(raw, wide):
    wide[...] = raw.astype(jnp.float32)


def narrow(wide, h, heads):
    return wide[pl.ds(h, wide.shape[0] // heads, stride=heads), :].astype(jnp.bfloat16)


def prefix_pass(load_q, kd, vd, acc, den, top, at, scale, arrive):
    heads, plen, hd = kd.shape
    part = min(plen, 1024)
    pieces = plen // part
    stages = [(h, c) for h in range(heads) for c in range(pieces)]

    def score(stage):
        h, c = stage
        if c == 0:
            arrive(h)
        return nt_dot(load_q(h), kd[h, pl.ds(c * part, part), :])

    ready = score(stages[0])
    held = []
    for index, (h, c) in enumerate(stages):
        s = ready
        if index + 1 < len(stages):
            ready = score(stages[index + 1])
        m = jnp.max(s, axis=1, keepdims=True) * scale
        p = jnp.exp2(s * scale - m).astype(jnp.bfloat16)
        v = vd[h, pl.ds(c * part, part), :]
        pv = jnp.dot(
            p, jnp.concatenate([v, jnp.ones_like(v)], axis=1),
            preferred_element_type=jnp.float32,
        )
        held.append((m, pv))
        if c == pieces - 1:
            m, pv = held[0]
            for m_more, pv_more in held[1:]:
                joined = jnp.maximum(m, m_more)
                pv = pv * jnp.exp2(m - joined) + pv_more * jnp.exp2(m_more - joined)
                m = joined
            held = []
            _, count, gs, _ = acc.shape
            shape = (pv.shape[0] // gs, gs, hd)
            acc[h, at] = pv[:, :hd].reshape(shape)
            den[h, at] = pv[:, hd:].reshape(shape)
            top[h, at] = jnp.broadcast_to(m, (pv.shape[0], hd)).reshape(shape)


def gather_kernel(
    q_hbm, k_hbm, v_hbm, qall, acc, den, top,
    kraw, vraw, kwide, vwide, kd, vd, own_sem, raw_sem, send_sem, recv_sem, *, n, scale, pieces
):
    p = lax.axis_index("prefix")
    rows, heads, gs, hd = q_hbm.shape
    flat = k_hbm.shape[0]
    piece = flat // pieces
    unit = kwide.shape[0]

    def raw_copies(i):
        at = pl.ds(i * piece, piece)
        return (
            pltpu.make_async_copy(k_hbm.at[at], kraw.at[at], raw_sem.at[0, i]),
            pltpu.make_async_copy(v_hbm.at[at], vraw.at[at], raw_sem.at[1, i]),
        )

    def block_at(b):
        return pl.ds(b * rows, rows)

    def own_copy(h):
        return pltpu.make_async_copy(q_hbm.at[:, h], qall.at[h, block_at(p)], own_sem.at[h])

    def send(src, side, b, h):
        return pltpu.make_async_remote_copy(
            src_ref=src,
            dst_ref=qall.at[h, block_at(b)],
            send_sem=send_sem.at[side, b, h],
            recv_sem=recv_sem.at[b, h],
            device_id={"prefix": p + 1 if side == 0 else p - 1},
            device_id_type=MESH,
        )

    for i in range(pieces):
        for copy in raw_copies(i):
            copy.start()
    for h in range(heads):
        own_copy(h).start()
    greet(p, n)
    outward = ((0, p < n - 1), (1, p > 0))
    for h in range(heads):
        for side, there in outward:

            @pl.when(there)
            def _(side=side, h=h):
                send(q_hbm.at[:, h], side, p, h).start()

    for i in range(pieces):
        for copy in raw_copies(i):
            copy.wait()

        def split(u, carry, i=i):
            at = pl.ds(pl.multiple_of(i * piece + u * unit, unit), unit)
            per = unit // heads
            to = pl.ds(pl.multiple_of(i * (piece // heads) + u * per, per), per)
            widen(kraw[at], kwide)
            widen(vraw[at], vwide)
            for h in range(heads):
                kd[h, to] = narrow(kwide, h, heads)
                vd[h, to] = narrow(vwide, h, heads)
            return carry

        lax.fori_loop(0, piece // unit, split, 0)

    near = jnp.minimum(p, n - 1 - p)
    longer = jnp.where(p > n - 1 - p, -1, 1)

    def body(k, carry):
        paired = p + jnp.where(k % 2 == 1, -1, 1) * ((k + 1) // 2)
        single = p + longer * (k - near)
        b = jnp.where(k <= 2 * near, paired, single)

        def arrive(h):
            @pl.when(k == 0)
            def _():
                own_copy(h).wait()

            for side, there in outward:
                source = p - k if side == 0 else p + k
                landed = qall.at[h, block_at(source)]

                @pl.when((k > 0) & (source >= 0) & (source < n))
                def _(side=side, source=source, landed=landed, there=there):
                    send(landed, side, source, h).wait_recv()

                    @pl.when(there)
                    def _():
                        send(landed, side, source, h).start()

        def load_q(h):
            return qall[h, block_at(b)].reshape(rows * gs, hd)

        prefix_pass(load_q, kd, vd, acc, den, top, block_at(b), scale, arrive)
        return carry

    lax.fori_loop(0, n, body, 0)

    def drain(k, carry):
        for h in range(heads):
            for side, there in outward:
                source = p - k if side == 0 else p + k

                @pl.when(there & (source >= 0) & (source < n))
                def _(side=side, source=source, h=h):
                    send(qall.at[h, block_at(source)], side, source, h).wait_send()

        return carry

    lax.fori_loop(0, n, drain, 0)


def gathered(q, kf, vf, n):
    rows, heads, gs, hd = q.shape
    flat = kf.shape[0]
    plen = flat // heads
    pieces = 4
    unit = min(1024, flat // pieces)
    everything = (heads, n * rows, gs, hd)
    state = jax.ShapeDtypeStruct(everything, jnp.float32)
    vmem = pl.BlockSpec(memory_space=pltpu.VMEM)
    hbm = pl.BlockSpec(memory_space=pltpu.HBM)
    dma = pltpu.SemaphoreType.DMA
    shapes = [jax.ShapeDtypeStruct(everything, jnp.bfloat16), state, state, state]
    return pl.pallas_call(
        functools.partial(gather_kernel, n=n, scale=LOG2E / math.sqrt(hd), pieces=pieces),
        in_specs=[hbm, hbm, hbm],
        out_specs=[vmem] * 4,
        out_shape=shapes,
        scratch_shapes=[
            pltpu.VMEM((flat, hd), jnp.bfloat16),
            pltpu.VMEM((flat, hd), jnp.bfloat16),
            pltpu.VMEM((unit, hd), jnp.float32),
            pltpu.VMEM((unit, hd), jnp.float32),
            pltpu.VMEM((heads, plen, hd), jnp.bfloat16),
            pltpu.VMEM((heads, plen, hd), jnp.bfloat16),
            dma((heads,)),
            dma((2, pieces)),
            dma((2, n, heads)),
            dma((n, heads)),
        ],
        compiler_params=pltpu.CompilerParams(
            collective_id=0, has_side_effects=True, vmem_limit_bytes=grant(*shapes)
        ),
    )(q, kf, vf)


def suffix_kernel(
    accepted, cache_slot, history, qall, acc_in, den_in, top_in, sk_hbm, sv_hbm,
    acc, den, top, kbuf, vbuf, kwide, vwide, kwide_b, vwide_b, kd, vd, kd_b, vd_b, meta, tasks, sems,
    *, scale
):
    owner = lax.axis_index("prefix")
    heads, count, gs, hd = qall.shape
    slots, flat, _ = sk_hbm.shape
    depth, wide, _ = kbuf.shape
    chunk = wide // heads
    window = MOST * gs

    def find(r, start):
        amount = accepted[r]
        slot = cache_slot[r] - owner * slots

        @pl.when((slot >= 0) & (slot < slots))
        def _():
            meta[slot, 0] = start
            meta[slot, 1] = amount
            meta[slot, 2] = history[r]

        return start + amount

    lax.fori_loop(0, accepted.shape[0], find, jnp.int32(0))

    def copies(task, buf):
        slot = tasks[task, 0]
        src = pl.ds(pl.multiple_of(tasks[task, 1] * wide, wide), wide)
        return (
            pltpu.make_async_copy(sk_hbm.at[slot, src], kbuf.at[buf], sems.at[0, buf]),
            pltpu.make_async_copy(sv_hbm.at[slot, src], vbuf.at[buf], sems.at[1, buf]),
        )

    total = jnp.int32(0)
    for slot in range(slots):
        blocks = (meta[slot, 1] + meta[slot, 2] + chunk - 1) // chunk

        def put(i, at, slot=slot):
            tasks[at, 0] = slot
            tasks[at, 1] = i
            return at + 1

        total = lax.fori_loop(0, blocks, put, total)

    def begin_copy(task):
        @pl.when(task < total)
        def _():
            for copy in copies(task, lax.rem(task, depth)):
                copy.start()

    def finish_copy(task):
        @pl.when(task < total)
        def _():
            for copy in copies(task, lax.rem(task, depth)):
                copy.wait()

    for task in range(depth - 1):
        begin_copy(jnp.int32(task))

    i_row = lax.broadcasted_iota(jnp.int32, (window, 1), 0) // gs
    pos = lax.broadcasted_iota(jnp.int32, (1, chunk), 1)
    shape = (MOST, gs, hd)

    def load(task, kwide, vwide):
        buf = lax.rem(task, depth)
        widen(kbuf[buf], kwide)
        widen(vbuf[buf], vwide)

    def spread(kwide, vwide, kd, vd):
        for h in range(heads):
            kd[h] = narrow(kwide, h, heads)
            vd[h] = narrow(vwide, h, heads)

    def attend(task, kd, vd):
        real = task < total
        known = jnp.minimum(task, total - 1)
        slot = tasks[known, 0]
        base = tasks[known, 1] * chunk
        begin = meta[slot, 0]
        amount = jnp.where(real, meta[slot, 1], 0)
        past = meta[slot, 2]
        start = jnp.minimum(begin, count - MOST)
        place = i_row + (start - begin)
        limit = jnp.where((place >= 0) & (place < amount), past + place + 1, 0) - base
        allowed = pos < limit
        rows_at = pl.ds(start, MOST)
        scores = [nt_dot(qall[h, rows_at].reshape(window, hd), kd[h]) for h in range(heads)]
        parts = []
        for h in range(heads):
            s = jnp.where(allowed, scores[h], NEG)
            m = jnp.maximum(jnp.max(s, axis=1, keepdims=True), FLOOR) * scale
            p = jnp.exp2(s * scale - m).astype(jnp.bfloat16)
            v = vd[h]
            pv = jnp.dot(
                p, jnp.concatenate([v, jnp.ones_like(v)], axis=1),
                preferred_element_type=jnp.float32,
            )
            parts.append((m, pv))
        for h, (m, pv) in enumerate(parts):
            old = top[h, rows_at].reshape(window, hd)
            new = jnp.maximum(old, m)
            keep = jnp.exp2(old - new)
            gain = jnp.exp2(m - new)
            top[h, rows_at] = new.reshape(shape)
            den[h, rows_at] = (
                den[h, rows_at].reshape(window, hd) * keep + pv[:, hd:] * gain
            ).reshape(shape)
            acc[h, rows_at] = (
                acc[h, rows_at].reshape(window, hd) * keep + pv[:, :hd] * gain
            ).reshape(shape)

    finish_copy(jnp.int32(0))
    load(jnp.int32(0), kwide, vwide)
    spread(kwide, vwide, kd, vd)

    def body(i, carry):
        t = 2 * i
        begin_copy(t + 3)
        begin_copy(t + 4)
        finish_copy(t + 1)
        finish_copy(t + 2)
        load(t + 1, kwide_b, vwide_b)
        attend(t, kd, vd)
        spread(kwide_b, vwide_b, kd_b, vd_b)
        load(t + 2, kwide, vwide)
        attend(t + 1, kd_b, vd_b)
        spread(kwide, vwide, kd, vd)
        return carry

    lax.fori_loop(0, (total + 1) // 2, body, 0)


def with_suffix(accepted, cache_slot, history, qall, acc, den, top, sk, sv):
    heads, count, gs, hd = qall.shape
    slots, flat, _ = sk.shape
    slen = flat // heads
    chunk = min(slen, 256)
    wide = chunk * heads
    depth = 4
    vmem = pl.BlockSpec(memory_space=pltpu.VMEM)
    hbm = pl.BlockSpec(memory_space=pltpu.HBM)
    smem = pl.BlockSpec(memory_space=pltpu.SMEM)
    return pl.pallas_call(
        functools.partial(suffix_kernel, scale=LOG2E / math.sqrt(hd)),
        in_specs=[smem] * 3 + [vmem] * 4 + [hbm] * 2,
        out_specs=[vmem] * 3,
        out_shape=[jax.ShapeDtypeStruct(acc.shape, jnp.float32)] * 3,
        input_output_aliases={4: 0, 5: 1, 6: 2},
        scratch_shapes=[
            pltpu.VMEM((depth, wide, hd), jnp.bfloat16),
            pltpu.VMEM((depth, wide, hd), jnp.bfloat16),
        ]
        + [pltpu.VMEM((wide, hd), jnp.float32)] * 4
        + [pltpu.VMEM((heads, chunk, hd), jnp.bfloat16)] * 4
        + [
            pltpu.SMEM((slots, 3), jnp.int32),
            pltpu.SMEM((slots * (slen // chunk), 2), jnp.int32),
            pltpu.SemaphoreType.DMA((2, depth)),
        ],
        compiler_params=pltpu.CompilerParams(vmem_limit_bytes=grant(qall, acc, den, top)),
    )(accepted, cache_slot, history, qall, acc, den, top, sk, sv)


def reduce_kernel(
    acc, den, top, result, out_o, out_l, in_o, in_l, send_sem, recv_sem, *, n
):
    p = lax.axis_index("prefix")
    heads, count, gs, hd = acc.shape
    rows = count // n
    size = rows * gs
    groups = size // hd
    eye = lax.broadcasted_iota(jnp.int32, (1, hd, hd), 1) == lax.broadcasted_iota(
        jnp.int32, (1, hd, hd), 2
    )

    def sends(side, b, h):
        target = {"prefix": p + 1 if side == 0 else p - 1}
        return [
            pltpu.make_async_remote_copy(
                src_ref=out.at[b, h],
                dst_ref=into.at[side, b, h],
                send_sem=send_sem.at[kind, b, h],
                recv_sem=recv_sem.at[kind, side, b, h],
                device_id=target,
                device_id_type=MESH,
            )
            for kind, (out, into) in enumerate(((out_o, in_o), (out_l, in_l)))
        ]

    def own(b, h):
        at = pl.ds(b * rows, rows)
        return [ref[h, at].reshape(size, hd) for ref in (acc, den, top)]

    def joined(state, side, b, h):
        a, d, t = state
        o = in_o[side, b, h].astype(jnp.float32)
        lanes = jnp.broadcast_to(in_l[side, b, h][:, None, :], (groups, hd, hd))
        lse = jnp.sum(jnp.where(eye, lanes, 0.0), axis=2, keepdims=True).reshape(size, 1)
        m = jnp.maximum(t, lse)
        mine = jnp.exp2(t - m)
        theirs = jnp.exp2(lse - m)
        return a * mine + o * theirs, d * mine + theirs, m

    def pass_on(side, b, h, more):
        def emit(state):
            a, d, t = state
            out_o[b, h] = (a / d).astype(jnp.bfloat16)
            lse = (t + jnp.log2(d)).reshape(groups, hd, hd)
            out_l[b, h] = jnp.sum(jnp.where(eye, lse, 0.0), axis=1)

        @pl.when(more)
        def _():
            for copy in sends(side, b, h):
                copy.wait_recv()
            emit(joined(own(b, h), side, b, h))

        @pl.when(jnp.logical_not(more))
        def _():
            emit(own(b, h))

        for copy in sends(side, b, h):
            copy.start()

    greet(p, n)

    chunks = (n - 1) * heads

    def step(t, carry):
        right = t - STAGGER * p
        left = t - STAGGER * (n - 1 - p)
        ahead = n - 1 - right // heads
        behind = left // heads

        @pl.when((right >= 0) & (right < chunks) & (ahead > p))
        def _():
            pass_on(0, ahead, right % heads, p > 0)

        @pl.when((left >= 0) & (left < chunks) & (behind < p))
        def _():
            pass_on(1, behind, left % heads, p < n - 1)

        return carry

    lax.fori_loop(0, chunks + STAGGER * (n - 1), step, 0)

    def finish(state, h):
        a, d, _ = state
        result[:, h] = (a / d).astype(result.dtype).reshape(rows, gs, hd)

    for h in range(heads):
        for side, there in ((0, p > 0), (1, p < n - 1)):

            @pl.when(there)
            def _(side=side, h=h):
                for copy in sends(side, p, h):
                    copy.wait_recv()

        @pl.when((p > 0) & (p < n - 1))
        def _(h=h):
            finish(joined(joined(own(p, h), 0, p, h), 1, p, h), h)

        @pl.when((p > 0) & (p == n - 1))
        def _(h=h):
            finish(joined(own(p, h), 0, p, h), h)

        @pl.when((p == 0) & (p < n - 1))
        def _(h=h):
            finish(joined(own(p, h), 1, p, h), h)

    def drain(j, carry):
        for h in range(heads):

            @pl.when(n - 1 - j > p)
            def _(h=h):
                for copy in sends(0, n - 1 - j, h):
                    copy.wait_send()

            @pl.when(j < p)
            def _(h=h):
                for copy in sends(1, j, h):
                    copy.wait_send()

        return carry

    lax.fori_loop(0, n - 1, drain, 0)


def reduced(acc, den, top, n):
    heads, count, gs, hd = acc.shape
    rows = count // n
    size = rows * gs
    dma = pltpu.SemaphoreType.DMA
    return pl.pallas_call(
        functools.partial(reduce_kernel, n=n),
        out_shape=jax.ShapeDtypeStruct((rows, heads, gs, hd), jnp.bfloat16),
        scratch_shapes=[
            pltpu.VMEM((n, heads, size, hd), jnp.bfloat16),
            pltpu.VMEM((n, heads, size // hd, hd), jnp.float32),
            pltpu.VMEM((2, n, heads, size, hd), jnp.bfloat16),
            pltpu.VMEM((2, n, heads, size // hd, hd), jnp.float32),
            dma((2, n, heads)),
            dma((2, 2, n, heads)),
        ],
        compiler_params=pltpu.CompilerParams(
            collective_id=1, has_side_effects=True, vmem_limit_bytes=32 * 1024 * 1024
        ),
    )(acc, den, top)


def local(
    queries, prefix_keys, prefix_values, suffix_keys, suffix_values, accepted, cache_slot, history
):
    n = lax.axis_size("prefix")
    plen, heads, hd = prefix_keys.shape
    slots, slen, _, _ = suffix_keys.shape
    kf = prefix_keys.reshape(plen * heads, hd)
    vf = prefix_values.reshape(plen * heads, hd)
    sk = suffix_keys.reshape(slots, slen * heads, hd)
    sv = suffix_values.reshape(slots, slen * heads, hd)
    qall, acc, den, top = gathered(queries, kf, vf, n)
    acc, den, top = with_suffix(accepted, cache_slot, history, qall, acc, den, top, sk, sv)
    return reduced(acc, den, top, n)


def solution(mesh):
    in_specs = (
        P(("groups", "prefix"), "heads", "sub", None),
        P(("groups", "prefix"), "heads", None),
        P(("groups", "prefix"), "heads", None),
        P(("groups", "prefix"), None, "heads", None),
        P(("groups", "prefix"), None, "heads", None),
        P("groups"),
        P("groups"),
        P("groups"),
    )
    out_specs = P(("groups", "prefix"), "heads", "sub", None)
    return jax.shard_map(local, mesh=mesh, in_specs=in_specs, out_specs=out_specs, check_vma=False)
```

```python
import functools
import math

import jax
import jax.numpy as jnp
from jax import lax
from jax.experimental import pallas as pl
from jax.experimental.pallas import tpu as pltpu
from jax.sharding import PartitionSpec as P

MOST = 8
NEG = -1e30
FLOOR = -1e29
LOG2E = 1.4426950408889634
VMEM = 67043328
STAGGER = 2
BATCH = 4
LOOK = 2
SPARE = 12 * 1024 * 1024
MESH = pl.DeviceIdType.MESH


def nt_dot(a, b):
    return lax.dot_general(a, b, (((1,), (1,)), ((), ())), preferred_element_type=jnp.float32)


def greet(p, n):
    barrier = pltpu.get_barrier_semaphore()
    for step, there in ((-1, p > 0), (1, p < n - 1)):

        @pl.when(there)
        def _(step=step):
            pl.semaphore_signal(
                barrier, inc=1, device_id={"prefix": p + step}, device_id_type=MESH
            )

    pl.semaphore_wait(barrier, jnp.minimum(p, 1) + jnp.minimum(n - 1 - p, 1))


def grant(*held):
    kept = sum(math.prod(x.shape) * jnp.dtype(x.dtype).itemsize for x in held)
    return VMEM - kept - SPARE


def widen(raw, wide):
    wide[...] = raw.astype(jnp.float32)


def narrow(wide, h, heads):
    return wide[pl.ds(h, wide.shape[0] // heads, stride=heads), :].astype(jnp.bfloat16)


def prefix_pass(load_q, kd, vd, acc, den, top, at, scale, arrive):
    heads, plen, hd = kd.shape
    part = min(plen, 1024)
    pieces = plen // part
    stages = [(h, c) for h in range(heads) for c in range(pieces)]

    def score(stage):
        h, c = stage
        if c == 0:
            arrive(h)
        return nt_dot(load_q(h), kd[h, pl.ds(c * part, part), :])

    ready = score(stages[0])
    held = []
    for index, (h, c) in enumerate(stages):
        s = ready
        if index + 1 < len(stages):
            ready = score(stages[index + 1])
        m = jnp.max(s, axis=1, keepdims=True) * scale
        p = jnp.exp2(s * scale - m).astype(jnp.bfloat16)
        v = vd[h, pl.ds(c * part, part), :]
        pv = jnp.dot(
            p, jnp.concatenate([v, jnp.ones_like(v)], axis=1),
            preferred_element_type=jnp.float32,
        )
        held.append((m, pv))
        if c == pieces - 1:
            m, pv = held[0]
            for m_more, pv_more in held[1:]:
                joined = jnp.maximum(m, m_more)
                pv = pv * jnp.exp2(m - joined) + pv_more * jnp.exp2(m_more - joined)
                m = joined
            held = []
            _, count, gs, _ = acc.shape
            shape = (pv.shape[0] // gs, gs, hd)
            acc[h, at] = pv[:, :hd].reshape(shape)
            den[h, at] = pv[:, hd:].reshape(shape)
            top[h, at] = jnp.broadcast_to(m, (pv.shape[0], hd)).reshape(shape)


def gather_kernel(
    q_hbm, k_hbm, v_hbm, qall, acc, den, top,
    kraw, vraw, kwide, vwide, kd, vd, own_sem, raw_sem, send_sem, recv_sem, *, n, scale, pieces
):
    p = lax.axis_index("prefix")
    rows, heads, gs, hd = q_hbm.shape
    flat = k_hbm.shape[0]
    piece = flat // pieces
    unit = kwide.shape[0]

    def raw_copies(i):
        at = pl.ds(i * piece, piece)
        return (
            pltpu.make_async_copy(k_hbm.at[at], kraw.at[at], raw_sem.at[0, i]),
            pltpu.make_async_copy(v_hbm.at[at], vraw.at[at], raw_sem.at[1, i]),
        )

    def block_at(b):
        return pl.ds(b * rows, rows)

    def own_copy(h):
        return pltpu.make_async_copy(q_hbm.at[:, h], qall.at[h, block_at(p)], own_sem.at[h])

    def send(src, side, b, h):
        return pltpu.make_async_remote_copy(
            src_ref=src,
            dst_ref=qall.at[h, block_at(b)],
            send_sem=send_sem.at[side, b, h],
            recv_sem=recv_sem.at[b, h],
            device_id={"prefix": p + 1 if side == 0 else p - 1},
            device_id_type=MESH,
        )

    for i in range(pieces):
        for copy in raw_copies(i):
            copy.start()
    for h in range(heads):
        own_copy(h).start()
    greet(p, n)
    outward = ((0, p < n - 1), (1, p > 0))
    for h in range(heads):
        for side, there in outward:

            @pl.when(there)
            def _(side=side, h=h):
                send(q_hbm.at[:, h], side, p, h).start()

    for i in range(pieces):
        for copy in raw_copies(i):
            copy.wait()

        def split(u, carry, i=i):
            at = pl.ds(pl.multiple_of(i * piece + u * unit, unit), unit)
            per = unit // heads
            to = pl.ds(pl.multiple_of(i * (piece // heads) + u * per, per), per)
            widen(kraw[at], kwide)
            widen(vraw[at], vwide)
            for h in range(heads):
                kd[h, to] = narrow(kwide, h, heads)
                vd[h, to] = narrow(vwide, h, heads)
            return carry

        lax.fori_loop(0, piece // unit, split, 0)

    near = jnp.minimum(p, n - 1 - p)
    longer = jnp.where(p > n - 1 - p, -1, 1)

    def body(k, carry):
        paired = p + jnp.where(k % 2 == 1, -1, 1) * ((k + 1) // 2)
        single = p + longer * (k - near)
        b = jnp.where(k <= 2 * near, paired, single)

        def arrive(h):
            @pl.when(k == 0)
            def _():
                own_copy(h).wait()

            for side, there in outward:
                source = p - k if side == 0 else p + k
                landed = qall.at[h, block_at(source)]

                @pl.when((k > 0) & (source >= 0) & (source < n))
                def _(side=side, source=source, landed=landed, there=there):
                    send(landed, side, source, h).wait_recv()

                    @pl.when(there)
                    def _():
                        send(landed, side, source, h).start()

        def load_q(h):
            return qall[h, block_at(b)].reshape(rows * gs, hd)

        prefix_pass(load_q, kd, vd, acc, den, top, block_at(b), scale, arrive)
        return carry

    lax.fori_loop(0, n, body, 0)

    def drain(k, carry):
        for h in range(heads):
            for side, there in outward:
                source = p - k if side == 0 else p + k

                @pl.when(there & (source >= 0) & (source < n))
                def _(side=side, source=source, h=h):
                    send(qall.at[h, block_at(source)], side, source, h).wait_send()

        return carry

    lax.fori_loop(0, n, drain, 0)


def gathered(q, kf, vf, n):
    rows, heads, gs, hd = q.shape
    flat = kf.shape[0]
    plen = flat // heads
    pieces = 4
    unit = min(1024, flat // pieces)
    everything = (heads, n * rows, gs, hd)
    state = jax.ShapeDtypeStruct(everything, jnp.float32)
    vmem = pl.BlockSpec(memory_space=pltpu.VMEM)
    hbm = pl.BlockSpec(memory_space=pltpu.HBM)
    dma = pltpu.SemaphoreType.DMA
    shapes = [jax.ShapeDtypeStruct(everything, jnp.bfloat16), state, state, state]
    return pl.pallas_call(
        functools.partial(gather_kernel, n=n, scale=LOG2E / math.sqrt(hd), pieces=pieces),
        in_specs=[hbm, hbm, hbm],
        out_specs=[vmem] * 4,
        out_shape=shapes,
        scratch_shapes=[
            pltpu.VMEM((flat, hd), jnp.bfloat16),
            pltpu.VMEM((flat, hd), jnp.bfloat16),
            pltpu.VMEM((unit, hd), jnp.float32),
            pltpu.VMEM((unit, hd), jnp.float32),
            pltpu.VMEM((heads, plen, hd), jnp.bfloat16),
            pltpu.VMEM((heads, plen, hd), jnp.bfloat16),
            dma((heads,)),
            dma((2, pieces)),
            dma((2, n, heads)),
            dma((n, heads)),
        ],
        compiler_params=pltpu.CompilerParams(
            collective_id=0, has_side_effects=True, vmem_limit_bytes=grant(*shapes)
        ),
    )(q, kf, vf)


def suffix_kernel(
    accepted, cache_slot, history, qall, acc_in, den_in, top_in, sk_hbm, sv_hbm,
    acc, den, top, kbuf, vbuf, kwide, vwide, kd, vd, meta, tasks, sems, *, scale
):
    owner = lax.axis_index("prefix")
    heads, count, gs, hd = qall.shape
    slots, flat, _ = sk_hbm.shape
    depth, wide, _ = kbuf.shape
    chunk = wide // heads
    window = MOST * gs

    def copies(task, buf):
        slot = tasks[task, 0]
        src = pl.ds(pl.multiple_of(tasks[task, 1] * wide, wide), wide)
        return (
            pltpu.make_async_copy(sk_hbm.at[slot, src], kbuf.at[buf], sems.at[0, buf]),
            pltpu.make_async_copy(sv_hbm.at[slot, src], vbuf.at[buf], sems.at[1, buf]),
        )

    for slot in range(slots):
        tasks[slot, 0] = slot
        tasks[slot, 1] = 0
        for copy in copies(slot, slot):
            copy.start()

    def find(r, start):
        amount = accepted[r]
        slot = cache_slot[r] - owner * slots

        @pl.when((slot >= 0) & (slot < slots))
        def _():
            meta[slot, 0] = start
            meta[slot, 1] = amount
            meta[slot, 2] = history[r]

        return start + amount

    lax.fori_loop(0, accepted.shape[0], find, jnp.int32(0))

    total = jnp.int32(slots)
    for slot in range(slots):
        blocks = (meta[slot, 1] + meta[slot, 2] + chunk - 1) // chunk

        def put(i, at, slot=slot):
            tasks[at, 0] = slot
            tasks[at, 1] = i
            return at + 1

        total = lax.fori_loop(1, blocks, put, total)

    def begin_copy(task):
        @pl.when(task < total)
        def _():
            for copy in copies(task, lax.rem(task, depth)):
                copy.start()

    def finish_copy(task):
        @pl.when(task < total)
        def _():
            for copy in copies(task, lax.rem(task, depth)):
                copy.wait()

    for task in range(slots, depth):
        begin_copy(jnp.int32(task))

    i_row = lax.broadcasted_iota(jnp.int32, (window, 1), 0) // gs
    pos = lax.broadcasted_iota(jnp.int32, (1, chunk), 1)
    shape = (MOST, gs, hd)

    def spread(task, k):
        buf = lax.rem(jnp.minimum(task, total - 1), depth)
        widen(kbuf[buf], kwide.at[k])
        widen(vbuf[buf], vwide.at[k])
        for h in range(heads):
            kd[k, h] = narrow(kwide.at[k], h, heads)
            vd[k, h] = narrow(vwide.at[k], h, heads)

    def place_of(task):
        known = jnp.minimum(task, total - 1)
        slot = tasks[known, 0]
        base = tasks[known, 1] * chunk
        begin = meta[slot, 0]
        amount = jnp.where(task < total, meta[slot, 1], 0)
        past = meta[slot, 2]
        start = jnp.minimum(begin, count - MOST)
        place = i_row + (start - begin)
        limit = jnp.where((place >= 0) & (place < amount), past + place + 1, 0) - base
        return pl.ds(start, MOST), limit

    def body(i, carry):
        first = i * BATCH
        for k in range(BATCH):
            finish_copy(first + k)
        for k in range(BATCH):
            spread(first + k, k)
        for k in range(BATCH):
            begin_copy(first + depth + k)
        spots = [place_of(first + k) for k in range(BATCH)]
        stages = [(k, h) for k in range(BATCH) for h in range(heads)]

        def score(stage):
            k, h = stage
            return nt_dot(qall[h, spots[k][0]].reshape(window, hd), kd[k, h])

        def fold(stage, m, pv):
            k, h = stage
            rows_at = spots[k][0]
            old = top[h, rows_at].reshape(window, hd)
            new = jnp.maximum(old, m)
            keep = jnp.exp2(old - new)
            gain = jnp.exp2(m - new)
            top[h, rows_at] = new.reshape(shape)
            den[h, rows_at] = (
                den[h, rows_at].reshape(window, hd) * keep + pv[:, hd:] * gain
            ).reshape(shape)
            acc[h, rows_at] = (
                acc[h, rows_at].reshape(window, hd) * keep + pv[:, :hd] * gain
            ).reshape(shape)

        ready = [score(stage) for stage in stages[:LOOK]]
        for index, (k, h) in enumerate(stages):
            if index + LOOK < len(stages):
                ready.append(score(stages[index + LOOK]))
            s = jnp.where(pos < spots[k][1], ready[index], NEG)
            m = jnp.maximum(jnp.max(s, axis=1, keepdims=True), FLOOR) * scale
            p = jnp.exp2(s * scale - m).astype(jnp.bfloat16)
            v = vd[k, h]
            pv = jnp.dot(
                p, jnp.concatenate([v, jnp.ones_like(v)], axis=1),
                preferred_element_type=jnp.float32,
            )
            fold((k, h), m, pv)
        return carry

    lax.fori_loop(0, (total + BATCH - 1) // BATCH, body, 0)


def with_suffix(accepted, cache_slot, history, qall, acc, den, top, sk, sv):
    heads, count, gs, hd = qall.shape
    slots, flat, _ = sk.shape
    slen = flat // heads
    chunk = min(slen, 256)
    wide = chunk * heads
    depth = slots + BATCH
    vmem = pl.BlockSpec(memory_space=pltpu.VMEM)
    hbm = pl.BlockSpec(memory_space=pltpu.HBM)
    smem = pl.BlockSpec(memory_space=pltpu.SMEM)
    return pl.pallas_call(
        functools.partial(suffix_kernel, scale=LOG2E / math.sqrt(hd)),
        in_specs=[smem] * 3 + [vmem] * 4 + [hbm] * 2,
        out_specs=[vmem] * 3,
        out_shape=[jax.ShapeDtypeStruct(acc.shape, jnp.float32)] * 3,
        input_output_aliases={4: 0, 5: 1, 6: 2},
        scratch_shapes=[
            pltpu.VMEM((depth, wide, hd), jnp.bfloat16),
            pltpu.VMEM((depth, wide, hd), jnp.bfloat16),
        ]
        + [pltpu.VMEM((BATCH, wide, hd), jnp.float32)] * 2
        + [pltpu.VMEM((BATCH, heads, chunk, hd), jnp.bfloat16)] * 2
        + [
            pltpu.SMEM((slots, 3), jnp.int32),
            pltpu.SMEM((slots * (slen // chunk), 2), jnp.int32),
            pltpu.SemaphoreType.DMA((2, depth)),
        ],
        compiler_params=pltpu.CompilerParams(vmem_limit_bytes=grant(qall, acc, den, top)),
    )(accepted, cache_slot, history, qall, acc, den, top, sk, sv)


def reduce_kernel(
    acc, den, top, result, out_o, out_l, in_o, in_l, send_sem, recv_sem, *, n
):
    p = lax.axis_index("prefix")
    heads, count, gs, hd = acc.shape
    rows = count // n
    size = rows * gs
    groups = size // hd
    eye = lax.broadcasted_iota(jnp.int32, (1, hd, hd), 1) == lax.broadcasted_iota(
        jnp.int32, (1, hd, hd), 2
    )

    def sends(side, b, h):
        target = {"prefix": p + 1 if side == 0 else p - 1}
        return [
            pltpu.make_async_remote_copy(
                src_ref=out.at[b, h],
                dst_ref=into.at[side, b, h],
                send_sem=send_sem.at[kind, b, h],
                recv_sem=recv_sem.at[kind, side, b, h],
                device_id=target,
                device_id_type=MESH,
            )
            for kind, (out, into) in enumerate(((out_o, in_o), (out_l, in_l)))
        ]

    def own(b, h):
        at = pl.ds(b * rows, rows)
        return [ref[h, at].reshape(size, hd) for ref in (acc, den, top)]

    def joined(state, side, b, h):
        a, d, t = state
        o = in_o[side, b, h].astype(jnp.float32)
        lanes = jnp.broadcast_to(in_l[side, b, h][:, None, :], (groups, hd, hd))
        lse = jnp.sum(jnp.where(eye, lanes, 0.0), axis=2, keepdims=True).reshape(size, 1)
        m = jnp.maximum(t, lse)
        mine = jnp.exp2(t - m)
        theirs = jnp.exp2(lse - m)
        return a * mine + o * theirs, d * mine + theirs, m

    def pass_on(side, b, h, more):
        def emit(state):
            a, d, t = state
            out_o[b, h] = (a / d).astype(jnp.bfloat16)
            lse = (t + jnp.log2(d)).reshape(groups, hd, hd)
            out_l[b, h] = jnp.sum(jnp.where(eye, lse, 0.0), axis=1)

        @pl.when(more)
        def _():
            for copy in sends(side, b, h):
                copy.wait_recv()
            emit(joined(own(b, h), side, b, h))

        @pl.when(jnp.logical_not(more))
        def _():
            emit(own(b, h))

        for copy in sends(side, b, h):
            copy.start()

    greet(p, n)

    chunks = (n - 1) * heads

    def step(t, carry):
        right = t - STAGGER * p
        left = t - STAGGER * (n - 1 - p)
        ahead = n - 1 - right // heads
        behind = left // heads

        @pl.when((right >= 0) & (right < chunks) & (ahead > p))
        def _():
            pass_on(0, ahead, right % heads, p > 0)

        @pl.when((left >= 0) & (left < chunks) & (behind < p))
        def _():
            pass_on(1, behind, left % heads, p < n - 1)

        return carry

    lax.fori_loop(0, chunks + STAGGER * (n - 1), step, 0)

    def finish(state, h):
        a, d, _ = state
        result[:, h] = (a / d).astype(result.dtype).reshape(rows, gs, hd)

    for h in range(heads):
        for side, there in ((0, p > 0), (1, p < n - 1)):

            @pl.when(there)
            def _(side=side, h=h):
                for copy in sends(side, p, h):
                    copy.wait_recv()

        @pl.when((p > 0) & (p < n - 1))
        def _(h=h):
            finish(joined(joined(own(p, h), 0, p, h), 1, p, h), h)

        @pl.when((p > 0) & (p == n - 1))
        def _(h=h):
            finish(joined(own(p, h), 0, p, h), h)

        @pl.when((p == 0) & (p < n - 1))
        def _(h=h):
            finish(joined(own(p, h), 1, p, h), h)

    def drain(j, carry):
        for h in range(heads):

            @pl.when(n - 1 - j > p)
            def _(h=h):
                for copy in sends(0, n - 1 - j, h):
                    copy.wait_send()

            @pl.when(j < p)
            def _(h=h):
                for copy in sends(1, j, h):
                    copy.wait_send()

        return carry

    lax.fori_loop(0, n - 1, drain, 0)


def reduced(acc, den, top, n):
    heads, count, gs, hd = acc.shape
    rows = count // n
    size = rows * gs
    dma = pltpu.SemaphoreType.DMA
    return pl.pallas_call(
        functools.partial(reduce_kernel, n=n),
        out_shape=jax.ShapeDtypeStruct((rows, heads, gs, hd), jnp.bfloat16),
        scratch_shapes=[
            pltpu.VMEM((n, heads, size, hd), jnp.bfloat16),
            pltpu.VMEM((n, heads, size // hd, hd), jnp.float32),
            pltpu.VMEM((2, n, heads, size, hd), jnp.bfloat16),
            pltpu.VMEM((2, n, heads, size // hd, hd), jnp.float32),
            dma((2, n, heads)),
            dma((2, 2, n, heads)),
        ],
        compiler_params=pltpu.CompilerParams(
            collective_id=1, has_side_effects=True, vmem_limit_bytes=32 * 1024 * 1024
        ),
    )(acc, den, top)


def local(
    queries, prefix_keys, prefix_values, suffix_keys, suffix_values, accepted, cache_slot, history
):
    n = lax.axis_size("prefix")
    plen, heads, hd = prefix_keys.shape
    slots, slen, _, _ = suffix_keys.shape
    kf = prefix_keys.reshape(plen * heads, hd)
    vf = prefix_values.reshape(plen * heads, hd)
    sk = suffix_keys.reshape(slots, slen * heads, hd)
    sv = suffix_values.reshape(slots, slen * heads, hd)
    qall, acc, den, top = gathered(queries, kf, vf, n)
    acc, den, top = with_suffix(accepted, cache_slot, history, qall, acc, den, top, sk, sv)
    return reduced(acc, den, top, n)


def solution(mesh):
    in_specs = (
        P(("groups", "prefix"), "heads", "sub", None),
        P(("groups", "prefix"), "heads", None),
        P(("groups", "prefix"), "heads", None),
        P(("groups", "prefix"), None, "heads", None),
        P(("groups", "prefix"), None, "heads", None),
        P("groups"),
        P("groups"),
        P("groups"),
    )
    out_specs = P(("groups", "prefix"), "heads", "sub", None)
    return jax.shard_map(local, mesh=mesh, in_specs=in_specs, out_specs=out_specs, check_vma=False)
```

```python
import functools
import math

import jax
import jax.numpy as jnp
from jax import lax
from jax.experimental import pallas as pl
from jax.experimental.pallas import tpu as pltpu
from jax.sharding import PartitionSpec as P

MOST = 8
NEG = -1e30
FLOOR = -1e29
LOG2E = 1.4426950408889634
VMEM = 67043328
STAGGER = 2
BATCH = 4
LOOK = 2
SPARE = 12 * 1024 * 1024
MESH = pl.DeviceIdType.MESH


def nt_dot(a, b):
    return lax.dot_general(a, b, (((1,), (1,)), ((), ())), preferred_element_type=jnp.float32)


def greet(p, n):
    barrier = pltpu.get_barrier_semaphore()
    for step, there in ((-1, p > 0), (1, p < n - 1)):

        @pl.when(there)
        def _(step=step):
            pl.semaphore_signal(
                barrier, inc=1, device_id={"prefix": p + step}, device_id_type=MESH
            )

    pl.semaphore_wait(barrier, jnp.minimum(p, 1) + jnp.minimum(n - 1 - p, 1))


def grant(*held):
    kept = sum(math.prod(x.shape) * jnp.dtype(x.dtype).itemsize for x in held)
    return VMEM - kept - SPARE


def widen(raw, wide):
    wide[...] = raw.astype(jnp.float32)


def narrow(wide, h, heads):
    return wide[pl.ds(h, wide.shape[0] // heads, stride=heads), :].astype(jnp.bfloat16)


def prefix_pass(load_q, kd, vd, acc, den, top, at, scale, arrive):
    heads, plen, hd = kd.shape
    part = min(plen, 1024)
    pieces = plen // part
    stages = [(h, c) for h in range(heads) for c in range(pieces)]

    def score(stage):
        h, c = stage
        if c == 0:
            arrive(h)
        return nt_dot(load_q(h), kd[h, pl.ds(c * part, part), :])

    ready = score(stages[0])
    held = []
    for index, (h, c) in enumerate(stages):
        s = ready
        if index + 1 < len(stages):
            ready = score(stages[index + 1])
        m = jnp.max(s, axis=1, keepdims=True) * scale
        p = jnp.exp2(s * scale - m).astype(jnp.bfloat16)
        v = vd[h, pl.ds(c * part, part), :]
        pv = jnp.dot(
            p, jnp.concatenate([v, jnp.ones_like(v)], axis=1),
            preferred_element_type=jnp.float32,
        )
        held.append((m, pv))
        if c == pieces - 1:
            m, pv = held[0]
            for m_more, pv_more in held[1:]:
                joined = jnp.maximum(m, m_more)
                pv = pv * jnp.exp2(m - joined) + pv_more * jnp.exp2(m_more - joined)
                m = joined
            held = []
            _, count, gs, _ = acc.shape
            shape = (pv.shape[0] // gs, gs, hd)
            acc[h, at] = pv[:, :hd].reshape(shape)
            den[h, at] = pv[:, hd:].reshape(shape)
            top[h, at] = jnp.broadcast_to(m, (pv.shape[0], hd)).reshape(shape)


def gather_kernel(
    q_hbm, k_hbm, v_hbm, qall, acc, den, top,
    kraw, vraw, kwide, vwide, kd, vd, own_sem, raw_sem, send_sem, recv_sem, *, n, scale, pieces
):
    p = lax.axis_index("prefix")
    rows, heads, gs, hd = q_hbm.shape
    flat = k_hbm.shape[0]
    piece = flat // pieces
    unit = kwide.shape[0]

    def raw_copies(i):
        at = pl.ds(i * piece, piece)
        return (
            pltpu.make_async_copy(k_hbm.at[at], kraw.at[at], raw_sem.at[0, i]),
            pltpu.make_async_copy(v_hbm.at[at], vraw.at[at], raw_sem.at[1, i]),
        )

    def block_at(b):
        return pl.ds(b * rows, rows)

    def own_copy(h):
        return pltpu.make_async_copy(q_hbm.at[:, h], qall.at[h, block_at(p)], own_sem.at[h])

    def send(src, side, b, h):
        return pltpu.make_async_remote_copy(
            src_ref=src,
            dst_ref=qall.at[h, block_at(b)],
            send_sem=send_sem.at[side, b, h],
            recv_sem=recv_sem.at[b, h],
            device_id={"prefix": p + 1 if side == 0 else p - 1},
            device_id_type=MESH,
        )

    for i in range(pieces):
        for copy in raw_copies(i):
            copy.start()
    for h in range(heads):
        own_copy(h).start()
    greet(p, n)
    outward = ((0, p < n - 1), (1, p > 0))
    for h in range(heads):
        for side, there in outward:

            @pl.when(there)
            def _(side=side, h=h):
                send(q_hbm.at[:, h], side, p, h).start()

    for i in range(pieces):
        for copy in raw_copies(i):
            copy.wait()

        def split(u, carry, i=i):
            at = pl.ds(pl.multiple_of(i * piece + u * unit, unit), unit)
            per = unit // heads
            to = pl.ds(pl.multiple_of(i * (piece // heads) + u * per, per), per)
            widen(kraw[at], kwide)
            widen(vraw[at], vwide)
            for h in range(heads):
                kd[h, to] = narrow(kwide, h, heads)
                vd[h, to] = narrow(vwide, h, heads)
            return carry

        lax.fori_loop(0, piece // unit, split, 0)

    near = jnp.minimum(p, n - 1 - p)
    longer = jnp.where(p > n - 1 - p, -1, 1)

    def body(k, carry):
        paired = p + jnp.where(k % 2 == 1, -1, 1) * ((k + 1) // 2)
        single = p + longer * (k - near)
        b = jnp.where(k <= 2 * near, paired, single)

        def arrive(h):
            @pl.when(k == 0)
            def _():
                own_copy(h).wait()

            for wave in (k, k + 1):
                lag = jnp.minimum(wave + 1, heads)
                c = (k - wave + 1) * heads + h - lag
                for side, there in outward:
                    source = p - wave if side == 0 else p + wave
                    due = (wave > 0) & (c >= 0) & (c < heads) & (source >= 0) & (source < n)

                    @pl.when(due)
                    def _(side=side, source=source, c=c, there=there):
                        landed = qall.at[c, block_at(source)]
                        send(landed, side, source, c).wait_recv()

                        @pl.when(there)
                        def _():
                            send(landed, side, source, c).start()

        def load_q(h):
            return qall[h, block_at(b)].reshape(rows * gs, hd)

        prefix_pass(load_q, kd, vd, acc, den, top, block_at(b), scale, arrive)
        return carry

    lax.fori_loop(0, n, body, 0)

    def drain(k, carry):
        for h in range(heads):
            for side, there in outward:
                source = p - k if side == 0 else p + k

                @pl.when(there & (source >= 0) & (source < n))
                def _(side=side, source=source, h=h):
                    send(qall.at[h, block_at(source)], side, source, h).wait_send()

        return carry

    lax.fori_loop(0, n, drain, 0)


def gathered(q, kf, vf, n):
    rows, heads, gs, hd = q.shape
    flat = kf.shape[0]
    plen = flat // heads
    pieces = 4
    unit = min(1024, flat // pieces)
    everything = (heads, n * rows, gs, hd)
    state = jax.ShapeDtypeStruct(everything, jnp.float32)
    vmem = pl.BlockSpec(memory_space=pltpu.VMEM)
    hbm = pl.BlockSpec(memory_space=pltpu.HBM)
    dma = pltpu.SemaphoreType.DMA
    shapes = [jax.ShapeDtypeStruct(everything, jnp.bfloat16), state, state, state]
    return pl.pallas_call(
        functools.partial(gather_kernel, n=n, scale=LOG2E / math.sqrt(hd), pieces=pieces),
        in_specs=[hbm, hbm, hbm],
        out_specs=[vmem] * 4,
        out_shape=shapes,
        scratch_shapes=[
            pltpu.VMEM((flat, hd), jnp.bfloat16),
            pltpu.VMEM((flat, hd), jnp.bfloat16),
            pltpu.VMEM((unit, hd), jnp.float32),
            pltpu.VMEM((unit, hd), jnp.float32),
            pltpu.VMEM((heads, plen, hd), jnp.bfloat16),
            pltpu.VMEM((heads, plen, hd), jnp.bfloat16),
            dma((heads,)),
            dma((2, pieces)),
            dma((2, n, heads)),
            dma((n, heads)),
        ],
        compiler_params=pltpu.CompilerParams(
            collective_id=0, has_side_effects=True, vmem_limit_bytes=grant(*shapes)
        ),
    )(q, kf, vf)


def suffix_kernel(
    accepted, cache_slot, history, qall, acc_in, den_in, top_in, sk_hbm, sv_hbm,
    acc, den, top, kbuf, vbuf, kwide, vwide, kd, vd, meta, tasks, sems, *, scale
):
    owner = lax.axis_index("prefix")
    heads, count, gs, hd = qall.shape
    slots, flat, _ = sk_hbm.shape
    depth, wide, _ = kbuf.shape
    chunk = wide // heads
    window = MOST * gs

    def copies(task, buf):
        slot = tasks[task, 0]
        src = pl.ds(pl.multiple_of(tasks[task, 1] * wide, wide), wide)
        return (
            pltpu.make_async_copy(sk_hbm.at[slot, src], kbuf.at[buf], sems.at[0, buf]),
            pltpu.make_async_copy(sv_hbm.at[slot, src], vbuf.at[buf], sems.at[1, buf]),
        )

    for slot in range(slots):
        tasks[slot, 0] = slot
        tasks[slot, 1] = 0
        for copy in copies(slot, slot):
            copy.start()

    def find(r, start):
        amount = accepted[r]
        slot = cache_slot[r] - owner * slots

        @pl.when((slot >= 0) & (slot < slots))
        def _():
            meta[slot, 0] = start
            meta[slot, 1] = amount
            meta[slot, 2] = history[r]

        return start + amount

    lax.fori_loop(0, accepted.shape[0], find, jnp.int32(0))

    total = jnp.int32(slots)
    for slot in range(slots):
        blocks = (meta[slot, 1] + meta[slot, 2] + chunk - 1) // chunk

        def put(i, at, slot=slot):
            tasks[at, 0] = slot
            tasks[at, 1] = i
            return at + 1

        total = lax.fori_loop(1, blocks, put, total)

    def begin_copy(task):
        @pl.when(task < total)
        def _():
            for copy in copies(task, lax.rem(task, depth)):
                copy.start()

    def finish_copy(task):
        @pl.when(task < total)
        def _():
            for copy in copies(task, lax.rem(task, depth)):
                copy.wait()

    for task in range(slots, depth):
        begin_copy(jnp.int32(task))

    i_row = lax.broadcasted_iota(jnp.int32, (window, 1), 0) // gs
    pos = lax.broadcasted_iota(jnp.int32, (1, chunk), 1)
    shape = (MOST, gs, hd)

    def spread(task, k):
        buf = lax.rem(jnp.minimum(task, total - 1), depth)
        widen(kbuf[buf], kwide.at[k])
        widen(vbuf[buf], vwide.at[k])
        for h in range(heads):
            kd[k, h] = narrow(kwide.at[k], h, heads)
            vd[k, h] = narrow(vwide.at[k], h, heads)

    def place_of(task):
        known = jnp.minimum(task, total - 1)
        slot = tasks[known, 0]
        base = tasks[known, 1] * chunk
        begin = meta[slot, 0]
        amount = jnp.where(task < total, meta[slot, 1], 0)
        past = meta[slot, 2]
        start = jnp.minimum(begin, count - MOST)
        place = i_row + (start - begin)
        limit = jnp.where((place >= 0) & (place < amount), past + place + 1, 0) - base
        return pl.ds(start, MOST), limit

    def body(i, carry):
        first = i * BATCH
        for k in range(BATCH):
            finish_copy(first + k)
        for k in range(BATCH):
            spread(first + k, k)
        for k in range(BATCH):
            begin_copy(first + depth + k)
        spots = [place_of(first + k) for k in range(BATCH)]
        stages = [(k, h) for k in range(BATCH) for h in range(heads)]

        def score(stage):
            k, h = stage
            return nt_dot(qall[h, spots[k][0]].reshape(window, hd), kd[k, h])

        def fold(stage, m, pv):
            k, h = stage
            rows_at = spots[k][0]
            old = top[h, rows_at].reshape(window, hd)
            new = jnp.maximum(old, m)
            keep = jnp.exp2(old - new)
            gain = jnp.exp2(m - new)
            top[h, rows_at] = new.reshape(shape)
            den[h, rows_at] = (
                den[h, rows_at].reshape(window, hd) * keep + pv[:, hd:] * gain
            ).reshape(shape)
            acc[h, rows_at] = (
                acc[h, rows_at].reshape(window, hd) * keep + pv[:, :hd] * gain
            ).reshape(shape)

        ready = [score(stage) for stage in stages[:LOOK]]
        for index, (k, h) in enumerate(stages):
            if index + LOOK < len(stages):
                ready.append(score(stages[index + LOOK]))
            s = jnp.where(pos < spots[k][1], ready[index], NEG)
            m = jnp.maximum(jnp.max(s, axis=1, keepdims=True), FLOOR) * scale
            p = jnp.exp2(s * scale - m).astype(jnp.bfloat16)
            v = vd[k, h]
            pv = jnp.dot(
                p, jnp.concatenate([v, jnp.ones_like(v)], axis=1),
                preferred_element_type=jnp.float32,
            )
            fold((k, h), m, pv)
        return carry

    lax.fori_loop(0, (total + BATCH - 1) // BATCH, body, 0)


def with_suffix(accepted, cache_slot, history, qall, acc, den, top, sk, sv):
    heads, count, gs, hd = qall.shape
    slots, flat, _ = sk.shape
    slen = flat // heads
    chunk = min(slen, 256)
    wide = chunk * heads
    depth = slots + BATCH
    vmem = pl.BlockSpec(memory_space=pltpu.VMEM)
    hbm = pl.BlockSpec(memory_space=pltpu.HBM)
    smem = pl.BlockSpec(memory_space=pltpu.SMEM)
    return pl.pallas_call(
        functools.partial(suffix_kernel, scale=LOG2E / math.sqrt(hd)),
        in_specs=[smem] * 3 + [vmem] * 4 + [hbm] * 2,
        out_specs=[vmem] * 3,
        out_shape=[jax.ShapeDtypeStruct(acc.shape, jnp.float32)] * 3,
        input_output_aliases={4: 0, 5: 1, 6: 2},
        scratch_shapes=[
            pltpu.VMEM((depth, wide, hd), jnp.bfloat16),
            pltpu.VMEM((depth, wide, hd), jnp.bfloat16),
        ]
        + [pltpu.VMEM((BATCH, wide, hd), jnp.float32)] * 2
        + [pltpu.VMEM((BATCH, heads, chunk, hd), jnp.bfloat16)] * 2
        + [
            pltpu.SMEM((slots, 3), jnp.int32),
            pltpu.SMEM((slots * (slen // chunk), 2), jnp.int32),
            pltpu.SemaphoreType.DMA((2, depth)),
        ],
        compiler_params=pltpu.CompilerParams(vmem_limit_bytes=grant(qall, acc, den, top)),
    )(accepted, cache_slot, history, qall, acc, den, top, sk, sv)


def reduce_kernel(
    acc, den, top, result, out_o, out_l, in_o, in_l, send_sem, recv_sem, *, n
):
    p = lax.axis_index("prefix")
    heads, count, gs, hd = acc.shape
    rows = count // n
    size = rows * gs
    groups = size // hd
    eye = lax.broadcasted_iota(jnp.int32, (1, hd, hd), 1) == lax.broadcasted_iota(
        jnp.int32, (1, hd, hd), 2
    )

    def sends(side, b, h):
        target = {"prefix": p + 1 if side == 0 else p - 1}
        return [
            pltpu.make_async_remote_copy(
                src_ref=out.at[b, h],
                dst_ref=into.at[side, b, h],
                send_sem=send_sem.at[kind, b, h],
                recv_sem=recv_sem.at[kind, side, b, h],
                device_id=target,
                device_id_type=MESH,
            )
            for kind, (out, into) in enumerate(((out_o, in_o), (out_l, in_l)))
        ]

    def own(b, h):
        at = pl.ds(b * rows, rows)
        return [ref[h, at].reshape(size, hd) for ref in (acc, den, top)]

    def joined(state, side, b, h):
        a, d, t = state
        o = in_o[side, b, h].astype(jnp.float32)
        lanes = jnp.broadcast_to(in_l[side, b, h][:, None, :], (groups, hd, hd))
        lse = jnp.sum(jnp.where(eye, lanes, 0.0), axis=2, keepdims=True).reshape(size, 1)
        m = jnp.maximum(t, lse)
        mine = jnp.exp2(t - m)
        theirs = jnp.exp2(lse - m)
        return a * mine + o * theirs, d * mine + theirs, m

    def pass_on(side, b, h, more):
        def emit(state):
            a, d, t = state
            out_o[b, h] = (a / d).astype(jnp.bfloat16)
            lse = (t + jnp.log2(d)).reshape(groups, hd, hd)
            out_l[b, h] = jnp.sum(jnp.where(eye, lse, 0.0), axis=1)

        @pl.when(more)
        def _():
            for copy in sends(side, b, h):
                copy.wait_recv()
            emit(joined(own(b, h), side, b, h))

        @pl.when(jnp.logical_not(more))
        def _():
            emit(own(b, h))

        for copy in sends(side, b, h):
            copy.start()

    greet(p, n)

    chunks = (n - 1) * heads

    def step(t, carry):
        right = t - STAGGER * p
        left = t - STAGGER * (n - 1 - p)
        ahead = n - 1 - right // heads
        behind = left // heads

        @pl.when((right >= 0) & (right < chunks) & (ahead > p))
        def _():
            pass_on(0, ahead, right % heads, p > 0)

        @pl.when((left >= 0) & (left < chunks) & (behind < p))
        def _():
            pass_on(1, behind, left % heads, p < n - 1)

        return carry

    lax.fori_loop(0, chunks + STAGGER * (n - 1), step, 0)

    def finish(state, h):
        a, d, _ = state
        result[:, h] = (a / d).astype(result.dtype).reshape(rows, gs, hd)

    for h in range(heads):
        for side, there in ((0, p > 0), (1, p < n - 1)):

            @pl.when(there)
            def _(side=side, h=h):
                for copy in sends(side, p, h):
                    copy.wait_recv()

        @pl.when((p > 0) & (p < n - 1))
        def _(h=h):
            finish(joined(joined(own(p, h), 0, p, h), 1, p, h), h)

        @pl.when((p > 0) & (p == n - 1))
        def _(h=h):
            finish(joined(own(p, h), 0, p, h), h)

        @pl.when((p == 0) & (p < n - 1))
        def _(h=h):
            finish(joined(own(p, h), 1, p, h), h)

    def drain(j, carry):
        for h in range(heads):

            @pl.when(n - 1 - j > p)
            def _(h=h):
                for copy in sends(0, n - 1 - j, h):
                    copy.wait_send()

            @pl.when(j < p)
            def _(h=h):
                for copy in sends(1, j, h):
                    copy.wait_send()

        return carry

    lax.fori_loop(0, n - 1, drain, 0)


def reduced(acc, den, top, n):
    heads, count, gs, hd = acc.shape
    rows = count // n
    size = rows * gs
    dma = pltpu.SemaphoreType.DMA
    return pl.pallas_call(
        functools.partial(reduce_kernel, n=n),
        out_shape=jax.ShapeDtypeStruct((rows, heads, gs, hd), jnp.bfloat16),
        scratch_shapes=[
            pltpu.VMEM((n, heads, size, hd), jnp.bfloat16),
            pltpu.VMEM((n, heads, size // hd, hd), jnp.float32),
            pltpu.VMEM((2, n, heads, size, hd), jnp.bfloat16),
            pltpu.VMEM((2, n, heads, size // hd, hd), jnp.float32),
            dma((2, n, heads)),
            dma((2, 2, n, heads)),
        ],
        compiler_params=pltpu.CompilerParams(
            collective_id=1, has_side_effects=True, vmem_limit_bytes=32 * 1024 * 1024
        ),
    )(acc, den, top)


def local(
    queries, prefix_keys, prefix_values, suffix_keys, suffix_values, accepted, cache_slot, history
):
    n = lax.axis_size("prefix")
    plen, heads, hd = prefix_keys.shape
    slots, slen, _, _ = suffix_keys.shape
    kf = prefix_keys.reshape(plen * heads, hd)
    vf = prefix_values.reshape(plen * heads, hd)
    sk = suffix_keys.reshape(slots, slen * heads, hd)
    sv = suffix_values.reshape(slots, slen * heads, hd)
    qall, acc, den, top = gathered(queries, kf, vf, n)
    acc, den, top = with_suffix(accepted, cache_slot, history, qall, acc, den, top, sk, sv)
    return reduced(acc, den, top, n)


def solution(mesh):
    in_specs = (
        P(("groups", "prefix"), "heads", "sub", None),
        P(("groups", "prefix"), "heads", None),
        P(("groups", "prefix"), "heads", None),
        P(("groups", "prefix"), None, "heads", None),
        P(("groups", "prefix"), None, "heads", None),
        P("groups"),
        P("groups"),
        P("groups"),
    )
    out_specs = P(("groups", "prefix"), "heads", "sub", None)
    return jax.shard_map(local, mesh=mesh, in_specs=in_specs, out_specs=out_specs, check_vma=False)
```

```python
import functools
import math

import jax
import jax.numpy as jnp
from jax import lax
from jax.experimental import pallas as pl
from jax.experimental.pallas import tpu as pltpu
from jax.sharding import PartitionSpec as P

MOST = 8
NEG = -1e30
FLOOR = -1e29
LOG2E = 1.4426950408889634
VMEM = 67043328
STAGGER = 2
BATCH = 2
LOOK = 2
SPARE = 12 * 1024 * 1024
MESH = pl.DeviceIdType.MESH


def nt_dot(a, b):
    return lax.dot_general(a, b, (((1,), (1,)), ((), ())), preferred_element_type=jnp.float32)


def greet(p, n):
    barrier = pltpu.get_barrier_semaphore()
    for step, there in ((-1, p > 0), (1, p < n - 1)):

        @pl.when(there)
        def _(step=step):
            pl.semaphore_signal(
                barrier, inc=1, device_id={"prefix": p + step}, device_id_type=MESH
            )

    pl.semaphore_wait(barrier, jnp.minimum(p, 1) + jnp.minimum(n - 1 - p, 1))


def grant(*held):
    kept = sum(math.prod(x.shape) * jnp.dtype(x.dtype).itemsize for x in held)
    return VMEM - kept - SPARE


def widen(raw, wide):
    wide[...] = raw.astype(jnp.float32)


def narrow(wide, h, heads):
    return wide[pl.ds(h, wide.shape[0] // heads, stride=heads), :].astype(jnp.bfloat16)


def prefix_pass(load_q, kd, vd, acc, den, top, at, scale, arrive):
    heads, plen, hd = kd.shape
    part = min(plen, 1024)
    pieces = plen // part
    stages = [(h, c) for h in range(heads) for c in range(pieces)]

    def score(stage):
        h, c = stage
        if c == 0:
            arrive(h)
        return nt_dot(load_q(h), kd[h, pl.ds(c * part, part), :])

    ready = score(stages[0])
    held = []
    for index, (h, c) in enumerate(stages):
        s = ready
        if index + 1 < len(stages):
            ready = score(stages[index + 1])
        m = jnp.max(s, axis=1, keepdims=True) * scale
        p = jnp.exp2(s * scale - m).astype(jnp.bfloat16)
        v = vd[h, pl.ds(c * part, part), :]
        pv = jnp.dot(
            p, jnp.concatenate([v, jnp.ones_like(v)], axis=1),
            preferred_element_type=jnp.float32,
        )
        held.append((m, pv))
        if c == pieces - 1:
            m, pv = held[0]
            for m_more, pv_more in held[1:]:
                joined = jnp.maximum(m, m_more)
                pv = pv * jnp.exp2(m - joined) + pv_more * jnp.exp2(m_more - joined)
                m = joined
            held = []
            _, count, gs, _ = acc.shape
            shape = (pv.shape[0] // gs, gs, hd)
            acc[h, at] = pv[:, :hd].reshape(shape)
            den[h, at] = pv[:, hd:].reshape(shape)
            top[h, at] = jnp.broadcast_to(m, (pv.shape[0], hd)).reshape(shape)


def gather_kernel(
    q_hbm, k_hbm, v_hbm, qall, acc, den, top,
    kraw, vraw, kwide, vwide, kd, vd, own_sem, raw_sem, send_sem, recv_sem, *, n, scale, pieces
):
    p = lax.axis_index("prefix")
    rows, heads, gs, hd = q_hbm.shape
    flat = k_hbm.shape[0]
    piece = flat // pieces
    unit = kwide.shape[0]

    def raw_copies(i):
        at = pl.ds(i * piece, piece)
        return (
            pltpu.make_async_copy(k_hbm.at[at], kraw.at[at], raw_sem.at[0, i]),
            pltpu.make_async_copy(v_hbm.at[at], vraw.at[at], raw_sem.at[1, i]),
        )

    def block_at(b):
        return pl.ds(b * rows, rows)

    def own_copy(h):
        return pltpu.make_async_copy(q_hbm.at[:, h], qall.at[h, block_at(p)], own_sem.at[h])

    def send(src, side, b, h):
        return pltpu.make_async_remote_copy(
            src_ref=src,
            dst_ref=qall.at[h, block_at(b)],
            send_sem=send_sem.at[side, b, h],
            recv_sem=recv_sem.at[b, h],
            device_id={"prefix": p + 1 if side == 0 else p - 1},
            device_id_type=MESH,
        )

    for i in range(pieces):
        for copy in raw_copies(i):
            copy.start()
    for h in range(heads):
        own_copy(h).start()
    greet(p, n)
    outward = ((0, p < n - 1), (1, p > 0))
    for h in range(heads):
        for side, there in outward:

            @pl.when(there)
            def _(side=side, h=h):
                send(q_hbm.at[:, h], side, p, h).start()

    for i in range(pieces):
        for copy in raw_copies(i):
            copy.wait()

        def split(u, carry, i=i):
            at = pl.ds(pl.multiple_of(i * piece + u * unit, unit), unit)
            per = unit // heads
            to = pl.ds(pl.multiple_of(i * (piece // heads) + u * per, per), per)
            widen(kraw[at], kwide)
            widen(vraw[at], vwide)
            for h in range(heads):
                kd[h, to] = narrow(kwide, h, heads)
                vd[h, to] = narrow(vwide, h, heads)
            return carry

        lax.fori_loop(0, piece // unit, split, 0)

    near = jnp.minimum(p, n - 1 - p)
    longer = jnp.where(p > n - 1 - p, -1, 1)

    def body(k, carry):
        paired = p + jnp.where(k % 2 == 1, -1, 1) * ((k + 1) // 2)
        single = p + longer * (k - near)
        b = jnp.where(k <= 2 * near, paired, single)

        def arrive(h):
            @pl.when(k == 0)
            def _():
                own_copy(h).wait()

            for wave in (k, k + 1):
                lag = jnp.minimum(wave + 1, heads)
                c = (k - wave + 1) * heads + h - lag
                for side, there in outward:
                    source = p - wave if side == 0 else p + wave
                    due = (wave > 0) & (c >= 0) & (c < heads) & (source >= 0) & (source < n)

                    @pl.when(due)
                    def _(side=side, source=source, c=c, there=there):
                        landed = qall.at[c, block_at(source)]
                        send(landed, side, source, c).wait_recv()

                        @pl.when(there)
                        def _():
                            send(landed, side, source, c).start()

        def load_q(h):
            return qall[h, block_at(b)].reshape(rows * gs, hd)

        prefix_pass(load_q, kd, vd, acc, den, top, block_at(b), scale, arrive)
        return carry

    lax.fori_loop(0, n, body, 0)

    def drain(k, carry):
        for h in range(heads):
            for side, there in outward:
                source = p - k if side == 0 else p + k

                @pl.when(there & (source >= 0) & (source < n))
                def _(side=side, source=source, h=h):
                    send(qall.at[h, block_at(source)], side, source, h).wait_send()

        return carry

    lax.fori_loop(0, n, drain, 0)


def gathered(q, kf, vf, n):
    rows, heads, gs, hd = q.shape
    flat = kf.shape[0]
    plen = flat // heads
    pieces = 4
    unit = min(1024, flat // pieces)
    everything = (heads, n * rows, gs, hd)
    state = jax.ShapeDtypeStruct(everything, jnp.float32)
    vmem = pl.BlockSpec(memory_space=pltpu.VMEM)
    hbm = pl.BlockSpec(memory_space=pltpu.HBM)
    dma = pltpu.SemaphoreType.DMA
    shapes = [jax.ShapeDtypeStruct(everything, jnp.bfloat16), state, state, state]
    return pl.pallas_call(
        functools.partial(gather_kernel, n=n, scale=LOG2E / math.sqrt(hd), pieces=pieces),
        in_specs=[hbm, hbm, hbm],
        out_specs=[vmem] * 4,
        out_shape=shapes,
        scratch_shapes=[
            pltpu.VMEM((flat, hd), jnp.bfloat16),
            pltpu.VMEM((flat, hd), jnp.bfloat16),
            pltpu.VMEM((unit, hd), jnp.float32),
            pltpu.VMEM((unit, hd), jnp.float32),
            pltpu.VMEM((heads, plen, hd), jnp.bfloat16),
            pltpu.VMEM((heads, plen, hd), jnp.bfloat16),
            dma((heads,)),
            dma((2, pieces)),
            dma((2, n, heads)),
            dma((n, heads)),
        ],
        compiler_params=pltpu.CompilerParams(
            collective_id=0, has_side_effects=True, vmem_limit_bytes=grant(*shapes)
        ),
    )(q, kf, vf)


def suffix_kernel(
    accepted, cache_slot, history, qall, acc_in, den_in, top_in, sk_hbm, sv_hbm,
    acc, den, top, kbuf, vbuf, kwide, vwide, kd, vd, meta, tasks, sems, *, scale
):
    owner = lax.axis_index("prefix")
    heads, count, gs, hd = qall.shape
    slots, flat, _ = sk_hbm.shape
    depth, wide, _ = kbuf.shape
    chunk = wide // heads
    window = MOST * gs

    def copies(task, buf):
        slot = tasks[task, 0]
        src = pl.ds(pl.multiple_of(tasks[task, 1] * wide, wide), wide)
        return (
            pltpu.make_async_copy(sk_hbm.at[slot, src], kbuf.at[buf], sems.at[0, buf]),
            pltpu.make_async_copy(sv_hbm.at[slot, src], vbuf.at[buf], sems.at[1, buf]),
        )

    for slot in range(slots):
        tasks[slot, 0] = slot
        tasks[slot, 1] = 0
        for copy in copies(slot, slot):
            copy.start()

    def find(r, start):
        amount = accepted[r]
        slot = cache_slot[r] - owner * slots

        @pl.when((slot >= 0) & (slot < slots))
        def _():
            meta[slot, 0] = start
            meta[slot, 1] = amount
            meta[slot, 2] = history[r]

        return start + amount

    lax.fori_loop(0, accepted.shape[0], find, jnp.int32(0))

    total = jnp.int32(slots)
    for slot in range(slots):
        blocks = (meta[slot, 1] + meta[slot, 2] + chunk - 1) // chunk

        def put(i, at, slot=slot):
            tasks[at, 0] = slot
            tasks[at, 1] = i
            return at + 1

        total = lax.fori_loop(1, blocks, put, total)

    def begin_copy(task):
        @pl.when(task < total)
        def _():
            for copy in copies(task, lax.rem(task, depth)):
                copy.start()

    def finish_copy(task):
        @pl.when(task < total)
        def _():
            for copy in copies(task, lax.rem(task, depth)):
                copy.wait()

    for task in range(slots, depth):
        begin_copy(jnp.int32(task))

    i_row = lax.broadcasted_iota(jnp.int32, (window, 1), 0) // gs
    pos = lax.broadcasted_iota(jnp.int32, (1, chunk), 1)
    shape = (MOST, gs, hd)

    def spread(task, k):
        buf = lax.rem(jnp.minimum(task, total - 1), depth)
        widen(kbuf[buf], kwide.at[k])
        widen(vbuf[buf], vwide.at[k])
        for h in range(heads):
            kd[k, h] = narrow(kwide.at[k], h, heads)
            vd[k, h] = narrow(vwide.at[k], h, heads)

    def place_of(task):
        known = jnp.minimum(task, total - 1)
        slot = tasks[known, 0]
        base = tasks[known, 1] * chunk
        begin = meta[slot, 0]
        amount = jnp.where(task < total, meta[slot, 1], 0)
        past = meta[slot, 2]
        start = jnp.minimum(begin, count - MOST)
        place = i_row + (start - begin)
        limit = jnp.where((place >= 0) & (place < amount), past + place + 1, 0) - base
        return pl.ds(start, MOST), limit

    def body(i, carry):
        first = i * BATCH
        for k in range(BATCH):
            finish_copy(first + k)
        for k in range(BATCH):
            spread(first + k, k)
        for k in range(BATCH):
            begin_copy(first + depth + k)
        spots = [place_of(first + k) for k in range(BATCH)]
        stages = [(k, h) for k in range(BATCH) for h in range(heads)]

        def score(stage):
            k, h = stage
            return nt_dot(qall[h, spots[k][0]].reshape(window, hd), kd[k, h])

        def fold(stage, m, pv):
            k, h = stage
            rows_at = spots[k][0]
            old = top[h, rows_at].reshape(window, hd)
            new = jnp.maximum(old, m)
            keep = jnp.exp2(old - new)
            gain = jnp.exp2(m - new)
            top[h, rows_at] = new.reshape(shape)
            den[h, rows_at] = (
                den[h, rows_at].reshape(window, hd) * keep + pv[:, hd:] * gain
            ).reshape(shape)
            acc[h, rows_at] = (
                acc[h, rows_at].reshape(window, hd) * keep + pv[:, :hd] * gain
            ).reshape(shape)

        ready = [score(stage) for stage in stages[:LOOK]]
        for index, (k, h) in enumerate(stages):
            if index + LOOK < len(stages):
                ready.append(score(stages[index + LOOK]))
            s = jnp.where(pos < spots[k][1], ready[index], NEG)
            m = jnp.maximum(jnp.max(s, axis=1, keepdims=True), FLOOR) * scale
            p = jnp.exp2(s * scale - m).astype(jnp.bfloat16)
            v = vd[k, h]
            pv = jnp.dot(
                p, jnp.concatenate([v, jnp.ones_like(v)], axis=1),
                preferred_element_type=jnp.float32,
            )
            fold((k, h), m, pv)
        return carry

    lax.fori_loop(0, (total + BATCH - 1) // BATCH, body, 0)


def with_suffix(accepted, cache_slot, history, qall, acc, den, top, sk, sv):
    heads, count, gs, hd = qall.shape
    slots, flat, _ = sk.shape
    slen = flat // heads
    chunk = min(slen, 256)
    wide = chunk * heads
    depth = slots + 2 * BATCH
    vmem = pl.BlockSpec(memory_space=pltpu.VMEM)
    hbm = pl.BlockSpec(memory_space=pltpu.HBM)
    smem = pl.BlockSpec(memory_space=pltpu.SMEM)
    return pl.pallas_call(
        functools.partial(suffix_kernel, scale=LOG2E / math.sqrt(hd)),
        in_specs=[smem] * 3 + [vmem] * 4 + [hbm] * 2,
        out_specs=[vmem] * 3,
        out_shape=[jax.ShapeDtypeStruct(acc.shape, jnp.float32)] * 3,
        input_output_aliases={4: 0, 5: 1, 6: 2},
        scratch_shapes=[
            pltpu.VMEM((depth, wide, hd), jnp.bfloat16),
            pltpu.VMEM((depth, wide, hd), jnp.bfloat16),
        ]
        + [pltpu.VMEM((BATCH, wide, hd), jnp.float32)] * 2
        + [pltpu.VMEM((BATCH, heads, chunk, hd), jnp.bfloat16)] * 2
        + [
            pltpu.SMEM((slots, 3), jnp.int32),
            pltpu.SMEM((slots * (slen // chunk), 2), jnp.int32),
            pltpu.SemaphoreType.DMA((2, depth)),
        ],
        compiler_params=pltpu.CompilerParams(vmem_limit_bytes=grant(qall, acc, den, top)),
    )(accepted, cache_slot, history, qall, acc, den, top, sk, sv)


def reduce_kernel(
    acc, den, top, result, out_o, out_l, in_o, in_l, send_sem, recv_sem, *, n
):
    p = lax.axis_index("prefix")
    heads, count, gs, hd = acc.shape
    rows = count // n
    size = rows * gs
    groups = size // hd
    eye = lax.broadcasted_iota(jnp.int32, (1, hd, hd), 1) == lax.broadcasted_iota(
        jnp.int32, (1, hd, hd), 2
    )

    def sends(side, b, h):
        target = {"prefix": p + 1 if side == 0 else p - 1}
        return [
            pltpu.make_async_remote_copy(
                src_ref=out.at[b, h],
                dst_ref=into.at[side, b, h],
                send_sem=send_sem.at[kind, b, h],
                recv_sem=recv_sem.at[kind, side, b, h],
                device_id=target,
                device_id_type=MESH,
            )
            for kind, (out, into) in enumerate(((out_o, in_o), (out_l, in_l)))
        ]

    def own(b, h):
        at = pl.ds(b * rows, rows)
        return [ref[h, at].reshape(size, hd) for ref in (acc, den, top)]

    def joined(state, side, b, h):
        a, d, t = state
        o = in_o[side, b, h].astype(jnp.float32)
        lanes = jnp.broadcast_to(in_l[side, b, h][:, None, :], (groups, hd, hd))
        lse = jnp.sum(jnp.where(eye, lanes, 0.0), axis=2, keepdims=True).reshape(size, 1)
        m = jnp.maximum(t, lse)
        mine = jnp.exp2(t - m)
        theirs = jnp.exp2(lse - m)
        return a * mine + o * theirs, d * mine + theirs, m

    def pass_on(side, b, h, more):
        def emit(state):
            a, d, t = state
            out_o[b, h] = (a / d).astype(jnp.bfloat16)
            lse = (t + jnp.log2(d)).reshape(groups, hd, hd)
            out_l[b, h] = jnp.sum(jnp.where(eye, lse, 0.0), axis=1)

        @pl.when(more)
        def _():
            for copy in sends(side, b, h):
                copy.wait_recv()
            emit(joined(own(b, h), side, b, h))

        @pl.when(jnp.logical_not(more))
        def _():
            emit(own(b, h))

        for copy in sends(side, b, h):
            copy.start()

    greet(p, n)

    chunks = (n - 1) * heads

    def step(t, carry):
        right = t - STAGGER * p
        left = t - STAGGER * (n - 1 - p)
        ahead = n - 1 - right // heads
        behind = left // heads

        @pl.when((right >= 0) & (right < chunks) & (ahead > p))
        def _():
            pass_on(0, ahead, right % heads, p > 0)

        @pl.when((left >= 0) & (left < chunks) & (behind < p))
        def _():
            pass_on(1, behind, left % heads, p < n - 1)

        return carry

    lax.fori_loop(0, chunks + STAGGER * (n - 1), step, 0)

    def finish(state, h):
        a, d, _ = state
        result[:, h] = (a / d).astype(result.dtype).reshape(rows, gs, hd)

    for h in range(heads):
        for side, there in ((0, p > 0), (1, p < n - 1)):

            @pl.when(there)
            def _(side=side, h=h):
                for copy in sends(side, p, h):
                    copy.wait_recv()

        @pl.when((p > 0) & (p < n - 1))
        def _(h=h):
            finish(joined(joined(own(p, h), 0, p, h), 1, p, h), h)

        @pl.when((p > 0) & (p == n - 1))
        def _(h=h):
            finish(joined(own(p, h), 0, p, h), h)

        @pl.when((p == 0) & (p < n - 1))
        def _(h=h):
            finish(joined(own(p, h), 1, p, h), h)

    def drain(j, carry):
        for h in range(heads):

            @pl.when(n - 1 - j > p)
            def _(h=h):
                for copy in sends(0, n - 1 - j, h):
                    copy.wait_send()

            @pl.when(j < p)
            def _(h=h):
                for copy in sends(1, j, h):
                    copy.wait_send()

        return carry

    lax.fori_loop(0, n - 1, drain, 0)


def reduced(acc, den, top, n):
    heads, count, gs, hd = acc.shape
    rows = count // n
    size = rows * gs
    dma = pltpu.SemaphoreType.DMA
    return pl.pallas_call(
        functools.partial(reduce_kernel, n=n),
        out_shape=jax.ShapeDtypeStruct((rows, heads, gs, hd), jnp.bfloat16),
        scratch_shapes=[
            pltpu.VMEM((n, heads, size, hd), jnp.bfloat16),
            pltpu.VMEM((n, heads, size // hd, hd), jnp.float32),
            pltpu.VMEM((2, n, heads, size, hd), jnp.bfloat16),
            pltpu.VMEM((2, n, heads, size // hd, hd), jnp.float32),
            dma((2, n, heads)),
            dma((2, 2, n, heads)),
        ],
        compiler_params=pltpu.CompilerParams(
            collective_id=1, has_side_effects=True, vmem_limit_bytes=32 * 1024 * 1024
        ),
    )(acc, den, top)


def local(
    queries, prefix_keys, prefix_values, suffix_keys, suffix_values, accepted, cache_slot, history
):
    n = lax.axis_size("prefix")
    plen, heads, hd = prefix_keys.shape
    slots, slen, _, _ = suffix_keys.shape
    kf = prefix_keys.reshape(plen * heads, hd)
    vf = prefix_values.reshape(plen * heads, hd)
    sk = suffix_keys.reshape(slots, slen * heads, hd)
    sv = suffix_values.reshape(slots, slen * heads, hd)
    qall, acc, den, top = gathered(queries, kf, vf, n)
    acc, den, top = with_suffix(accepted, cache_slot, history, qall, acc, den, top, sk, sv)
    return reduced(acc, den, top, n)


def solution(mesh):
    in_specs = (
        P(("groups", "prefix"), "heads", "sub", None),
        P(("groups", "prefix"), "heads", None),
        P(("groups", "prefix"), "heads", None),
        P(("groups", "prefix"), None, "heads", None),
        P(("groups", "prefix"), None, "heads", None),
        P("groups"),
        P("groups"),
        P("groups"),
    )
    out_specs = P(("groups", "prefix"), "heads", "sub", None)
    return jax.shard_map(local, mesh=mesh, in_specs=in_specs, out_specs=out_specs, check_vma=False)
```
